512 devices in a mesh: band: 64 (over z, x), disp: 8 (over y, core).
Axes of the slice: x: 4, y: 4, z: 16, core: 2. Of those that a mesh axis runs over, the one named last changes fastest.
Arguments:
- feat_left: bfloat16 [64, 96, 1024], P('band', None, 'disp'), may hold values from -19 to 19
- feat_right: bfloat16 [64, 96, 1024], P('band', None, 'disp'), may hold values from -19 to 19
- limit: int32 [64, 1024], P('band', 'disp'), may hold values from 24 to 96
- indices: int32 [3, 64, 1024], P(None, 'band', 'disp'), may hold values from 0 to 95
- hidden_start: bfloat16 [64, 1024, 128], P('band', 'disp'), may hold values from -1 to 1
- vol_kernel: bfloat16 [3, 3, 3, 8, 8], replicated, may hold values from -0.4375 to 0.4375
- group_gain: float32 [8], replicated, may hold values from 0.5 to 2
- hid_kernel: bfloat16 [3, 3, 128, 384], replicated, may hold values from -0.1875 to 0.1875
- in_kernel: bfloat16 [3, 3, 9, 384], replicated, may hold values from -0.625 to 0.625
- head_weight: bfloat16 [128, 1], replicated, may hold values from -0.5 to 0.5
Outputs:
- disparity: float32 [64, 1024], P('band', 'disp')
- hidden: bfloat16 [64, 1024, 128], P('band', 'disp')
The draws below stay inside these ranges and needn't reach their ends.
All inputs are finite; a program needn't handle non-finite values.
Results may differ from the reference program's by a relative error of at most 0.007.
Values may be sent and summed in bfloat16 or wider, within the bound.
A program may use at most 128 MiB of HBM per device.

```python
import math
import jax
import jax.numpy as jnp
from jax import lax

ROWS_DEV = 1
FEAT_CH = 96
GROUPS = 8
DISPS = 96
HID_CH = 128
ITERS = 3
HEIGHT = 64
WIDTH = 1024


def feature_pair(key):
    left = jnp.clip(jax.random.normal(jax.random.fold_in(key, 11), (HEIGHT, FEAT_CH, WIDTH), jnp.float32), -6.0, 6.0)
    right = jnp.clip(jax.random.normal(jax.random.fold_in(key, 12), (HEIGHT, FEAT_CH, WIDTH), jnp.float32), -6.0, 6.0)
    return (left, right)


def draw_feat_left(key, part):
    return feature_pair(key)[0].astype(jnp.bfloat16)


def draw_feat_right(key, part):
    return feature_pair(key)[1].astype(jnp.bfloat16)


def touch_ends(array, stream_key, least, high):
    longest = array.shape.index(max(array.shape))
    spots = []
    for shift in (0, 1):
        where = [jax.random.randint(jax.random.fold_in(stream_key, axis), (), 0, length) for axis, length in enumerate(array.shape)]
        where[longest] = (where[longest] + shift) % array.shape[longest]
        spots.append(tuple(where))
    return array.at[spots[0]].set(least).at[spots[1]].set(high)


def steps_of(rng, shape, shards, least, largest):
    factor_of, own = 1.0, jax.random.fold_in(rng, 6)
    for axis_at, parts in shards:
        steps = jnp.exp(jax.random.uniform(jax.random.fold_in(own, axis_at), (parts,), jnp.float32, least / len(shards), largest / len(shards)))
        factor_of = factor_of * jnp.repeat(steps, shape[axis_at] // parts).reshape([-1 if axis == axis_at else 1 for axis in range(len(shape))])
    return factor_of


def gaussian(rng, dims, spread, reach, kind=jnp.bfloat16):
    drawn = spread * jax.random.normal(rng, dims, jnp.float32)
    return jnp.clip(drawn, min=-reach, max=reach).astype(kind)


def setup_inputs(seed: int = 0) -> dict:
    key_list = jax.random.split(jax.random.key(seed), 11)
    return {
        "feat_left": draw_feat_left(jax.random.fold_in(key_list[10], 71), 0),
        "feat_right": draw_feat_right(jax.random.fold_in(key_list[10], 71), 0),
        "limit": touch_ends(jax.random.randint(key_list[2], (HEIGHT, WIDTH), DISPS // 4, DISPS + 1), jax.random.fold_in(key_list[2], 1), DISPS // 4, DISPS).astype(jnp.int32),
        "indices": touch_ends(jax.random.randint(key_list[3], (ITERS, HEIGHT, WIDTH), 0, DISPS), jax.random.fold_in(key_list[3], 1), 0, DISPS - 1).astype(jnp.int32),
        "hidden_start": jnp.clip(jax.random.uniform(key_list[4], (HEIGHT, WIDTH, HID_CH), jnp.float32, -1.0, 1.0) * steps_of(key_list[4], (HEIGHT, WIDTH, HID_CH), ((0, 64), (1, 8)), -0.4, 0.0), -1.0, 1.0).astype(jnp.bfloat16),
        "vol_kernel": gaussian(key_list[5], (3, 3, 3, GROUPS, GROUPS), (27 * GROUPS) ** -0.5, 0.4375),
        "group_gain": jnp.clip(jnp.exp(jax.random.uniform(key_list[6], (GROUPS,), jnp.float32, math.log(0.5), math.log(2.0))), 0.5, 2.0),
        "hid_kernel": gaussian(key_list[7], (3, 3, HID_CH, 3 * HID_CH), (9 * HID_CH) ** -0.5, 0.1875),
        "in_kernel": gaussian(key_list[8], (3, 3, GROUPS + 1, 3 * HID_CH), (9 * (GROUPS + 1)) ** -0.5, 0.625),
        "head_weight": gaussian(key_list[9], (HID_CH, 1), HID_CH ** -0.5, 0.5),
    }


pixel_unit = 8.0
feature_scale = 0.25
floor_logit = -1e30


def correlate(left, right):
    row_count, channels, col_count = left.shape
    per_group = channels // GROUPS
    padded = jnp.pad(right, ((0, 0), (0, 0), (DISPS, 0)))

    def one_disp(offset):
        shifted = lax.dynamic_slice_in_dim(padded, (DISPS - offset).astype(jnp.int32), col_count, 2)
        products = left.astype(jnp.float32) * shifted.astype(jnp.float32)
        return products.reshape(row_count, GROUPS, per_group, col_count).sum(2) / per_group

    volume = lax.map(one_disp, jnp.arange(DISPS, dtype=jnp.int32))
    return volume.astype(jnp.bfloat16)


def conv_plane(values, kernel):
    result = lax.conv_general_dilated(values[None], kernel, (1, 1), ((1, 1), (1, 1)),
                                      dimension_numbers=("NHWC", "HWIO", "NHWC"),
                                      preferred_element_type=jnp.float32)
    return result[0]


def reference(feat_left, feat_right, limit, indices, hidden_start, vol_kernel, group_gain, hid_kernel, in_kernel, head_weight):
    left_pad = jnp.pad(feat_left, ((1, 1), (0, 0), (0, 0)))
    right_pad = jnp.pad(feat_right, ((1, 1), (0, 0), (0, 0)))
    levels = jnp.arange(DISPS, dtype=jnp.int32)[:, None, None]

    def band_block(band_index):
        first_row = band_index * ROWS_DEV
        left_rows = lax.dynamic_slice_in_dim(left_pad, first_row, ROWS_DEV + 2, 0)
        right_rows = lax.dynamic_slice_in_dim(right_pad, first_row, ROWS_DEV + 2, 0)
        raw_volume = correlate(left_rows, right_rows).transpose(0, 1, 3, 2)
        conv_out = lax.conv_general_dilated(raw_volume[None], vol_kernel, (1, 1, 1), ((1, 1), (0, 0), (1, 1)),
                                            dimension_numbers=("NDHWC", "DHWIO", "NDHWC"),
                                            preferred_element_type=jnp.float32)[0]
        volume = (raw_volume[:, 1:-1].astype(jnp.float32) + jnp.maximum(conv_out, 0.0)).astype(jnp.bfloat16)
        logits = jnp.sum(volume.astype(jnp.float32) * group_gain, axis=-1)
        limit_rows = lax.dynamic_slice_in_dim(limit, first_row, ROWS_DEV, 0)
        valid = levels < limit_rows[None]
        masked = jnp.where(valid, logits, floor_logit)
        row_top = jnp.max(masked, axis=0)
        weights = jnp.where(valid, jnp.exp(masked - row_top), 0.0)
        moment = jnp.sum(weights * levels.astype(jnp.float32), axis=0)
        initial = moment / jnp.sum(weights, axis=0) / pixel_unit
        index_rows = lax.dynamic_slice_in_dim(indices, first_row, ROWS_DEV, 1)
        lookups = []
        for iteration in range(ITERS):
            where_at = jnp.broadcast_to(index_rows[iteration][None, :, :, None], (1,) + volume.shape[1:])
            lookups.append(jnp.take_along_axis(volume, where_at, axis=0)[0])
        return initial, jnp.stack(lookups)

    initial, lookups = lax.map(band_block, jnp.arange(HEIGHT // ROWS_DEV, dtype=jnp.int32))
    disparity = initial.reshape(HEIGHT, WIDTH)
    lookups = lookups.transpose(1, 0, 2, 3, 4).reshape(ITERS, HEIGHT, WIDTH, GROUPS)
    hidden = hidden_start
    for iteration in range(ITERS):
        inputs = jnp.concatenate([lookups[iteration].astype(jnp.float32), (feature_scale * disparity)[..., None]], -1).astype(jnp.bfloat16)
        in_conv = conv_plane(inputs, in_kernel)
        hid_conv = conv_plane(hidden, hid_kernel[:, :, :, :2 * HID_CH])
        update = jax.nn.sigmoid(hid_conv[..., :HID_CH] + in_conv[..., :HID_CH])
        reset_gate = jax.nn.sigmoid(hid_conv[..., HID_CH:] + in_conv[..., HID_CH:2 * HID_CH])
        reset_hidden = (reset_gate * hidden.astype(jnp.float32)).astype(jnp.bfloat16)
        candidate = jnp.tanh(conv_plane(reset_hidden, hid_kernel[:, :, :, 2 * HID_CH:]) + in_conv[..., 2 * HID_CH:])
        hidden = ((1.0 - update) * hidden.astype(jnp.float32) + update * candidate).astype(jnp.bfloat16)
        change = jnp.dot(hidden.reshape(-1, HID_CH), head_weight, preferred_element_type=jnp.float32)
        disparity = disparity + change.reshape(HEIGHT, WIDTH)
    return disparity, hidden
```

```python
import jax
import jax.numpy as jnp
from jax import lax
from jax.experimental import pallas as pl
from jax.experimental.pallas import tpu as pltpu
from jax.sharding import PartitionSpec as P

GROUPS = 8
DISPS = 96
PER_GROUP = 12
CH = 96
HID = 128
ITERS = 3
COLS = 128

MESH = pl.DeviceIdType.MESH
F32 = jnp.float32
BF16 = jnp.bfloat16

AROUND = [(r, c) for r in range(-2, 3) for c in (-1, 0, 1) if (r, c) != (0, 0)]
BLOCK = 14
PAIRS = 50
EXT = COLS + 16
NT = (((1,), (1,)), ((), ()))


def dot(a, b):
    return jnp.dot(a, b, preferred_element_type=F32)


def dot_nt(a, b):
    return lax.dot_general(a, b, NT, preferred_element_type=F32)


def iota(shape, dim):
    return lax.broadcasted_iota(jnp.int32, shape, dim)


def one_hot(cond):
    return jnp.where(cond, 1.0, 0.0).astype(BF16)


def kernel(
    gain_ref, fl_in, fr_in, lim_in, ind_in, h0_in, vk_in, hk_in, ik_in, hw_in,
    disp_out, hid_out,
    fl, fr, fp, edge, edge_l, edge_r, lim, ind, vk, ik, hw,
    lp, rc, rp, el, er, ins, tw, lg,
    hr, hl, hrt, lm, hf, rf, dd, lk3, x4, xr, w4, win, ikf,
    local_sem, feat_send, feat_recv, hid_send, hid_recv, look_send, look_recv,
):
    band, disp = lax.axis_index("band"), lax.axis_index("disp")
    bands, disps = lax.axis_size("band"), lax.axis_size("disp")

    def device(r, c):
        return (lax.rem(band + r + bands, bands), lax.rem(disp + c + disps, disps))

    locals_ = [
        pltpu.make_async_copy(src, dst, local_sem.at[i])
        for i, (src, dst) in enumerate(
            [
                (fl_in, fl.at[1]),
                (fr_in, fr.at[1]),
                (vk_in, vk),
                (ik_in, ik),
                (hw_in, hw),
                (lim_in, lim),
                (ind_in, ind),
                (h0_in, hr.at[0, 2]),
                (hk_in, w4.at[:, 0:384, :]),
            ]
        )
    ]
    for copy in locals_:
        copy.start()

    barrier = pltpu.get_barrier_semaphore()
    for r, c in AROUND:
        pl.semaphore_signal(barrier, inc=1, device_id=device(r, c), device_id_type=MESH)

    locals_[0].wait()
    locals_[1].wait()
    pad = jnp.zeros((32, COLS), BF16)
    row16, lane16 = iota((16, COLS), 0), iota((16, COLS), 1)
    pick_left = one_hot(((row16 == 0) & (lane16 == 0)) | ((row16 == 2) & (lane16 == COLS - 1)))
    pick_right = one_hot((row16 == 1) & (lane16 == 0))
    edge[...] = (
        dot_nt(pick_left, jnp.concatenate([fl[1], pad], 0))
        + dot_nt(pick_right, jnp.concatenate([fr[1], pad], 0))
    ).astype(BF16)

    pl.semaphore_wait(barrier, len(AROUND))

    def remote(src, dst, send, recv, i, r, c):
        return pltpu.make_async_remote_copy(
            src_ref=src, dst_ref=dst, send_sem=send.at[i], recv_sem=recv.at[i],
            device_id=device(r, c), device_id_type=MESH,
        )

    feats = {}
    plan = [(r, -1, "p") for r in (0, -1, 1)] + [(r, -1, "e") for r in (0, -1, 1)]
    plan += [(r, 1, "e") for r in (0, -1, 1)]
    plan += [(r, 0, kind) for r in (-1, 1) for kind in ("l", "r")]
    for i, (r, c, kind) in enumerate(plan):
        src, dst = {
            "p": (fr_in, fp.at[r + 1]),
            "e": (edge, (edge_l if c < 0 else edge_r).at[r + 1]),
            "l": (fl_in, fl.at[r + 1]),
            "r": (fr_in, fr.at[r + 1]),
        }[kind]
        feats[(r, c, kind)] = remote(src, dst, feat_send, feat_recv, i, -r, -c)
        feats[(r, c, kind)].start()

    def hidden_copies(t):
        copies = []
        for i, (r, c) in enumerate(AROUND):
            own = h0_in if t == 0 else hr.at[t, 2]
            if c == 0:
                src, dst = own, hr.at[t, r + 2]
            elif c < 0:
                src, dst = own.at[COLS - 16 : COLS], hl.at[t, r + 2]
            else:
                src, dst = own.at[0:16], hrt.at[t, r + 2]
            copies.append(
                remote(src, dst, hid_send.at[t], hid_recv.at[t], i, -r, -c)
            )
        return copies

    hidden_sent = [hidden_copies(0)]
    for copy in hidden_sent[0]:
        copy.start()

    for copy in locals_[2:]:
        copy.wait()
    lane8 = iota((8, COLS), 1)
    spread = one_hot(iota((8, COLS), 0) == lax.rem(lane8, 8))
    taps = dot(vk[...], spread)
    lane_disp = lane8 // 8
    eye = one_hot(iota((128, 128), 0) == iota((128, 128), 1))
    for b in range(3):
        for e in range(3):
            tap = [taps[((a * 3 + b) * 3 + e) * 8 :][:8] for a in range(3)]
            rows = []
            for at in range(16):
                block = jnp.zeros((8, COLS), F32)
                for a in range(3):
                    block = jnp.where(lane_disp == at - a, tap[a], block)
                rows.append(block)
            toeplitz = jnp.concatenate(rows, 0).astype(BF16)
            slot = (b * 3 + e) * 128
            tw[:, slot : slot + 128] = dot_nt(eye, toeplitz).astype(BF16)

    head_rows = jnp.broadcast_to(hw[...].astype(F32), (128, HID)).astype(BF16)
    head = dot_nt(eye, head_rows).astype(BF16)
    head_row = head_rows[0:16]

    ikf[...] = jnp.zeros_like(ikf)
    for a in range(3):
        for i in range(GROUPS + 1):
            ikf[a, 3 * i : 3 * i + 3, :] = ik[a, i].astype(F32)
    source = iota((128, 32), 1)
    source_i, source_b = source // 3, lax.rem(source, 3)
    for t in range(ITERS):
        goes_to = 32 * source_b + jnp.where(source_i < GROUPS, 8 * t + source_i, 24)
        move = one_hot((source < 27) & (iota((128, 32), 0) == goes_to))
        for a in range(3):
            win[t, a] = dot(move, ikf[a].astype(BF16)).astype(BF16)

    hf[...] = jnp.zeros_like(hf)
    rf[...] = jnp.zeros_like(rf)
    dd[...] = jnp.zeros_like(dd)

    row_ok = {r: (band + r >= 0) & (band + r < bands) for r in range(-2, 3)}
    left_ok, right_ok = disp > 0, disp < disps - 1

    def flag(ok):
        return jnp.where(ok, 1.0, 0.0).astype(F32)

    chan = iota((CH, 128), 0)
    perm = one_hot(iota((CH, 128), 1) == lax.rem(chan, 8) * PER_GROUP + chan // 8)
    perm_ch = one_hot(
        iota((CH, CH), 1) == lax.rem(iota((CH, CH), 0), 8) * PER_GROUP + iota((CH, CH), 0) // 8
    )

    def prepare(b):
        lp[b] = dot(perm_ch, fl[b])
        rc[b] = dot(perm_ch, fr[b])
        rp[b] = dot(perm_ch, fp[b]) * flag(left_ok)

        def column(ref, row):
            line = ref[b].astype(F32)[row : row + 1]
            return dot_nt(perm, jnp.broadcast_to(line, (128, 128)).astype(BF16))

        left_col, right_col, right_right = column(edge_l, 2), column(edge_r, 0), column(edge_r, 1)
        left_sum = jnp.zeros((8, COLS), F32)
        right_sum = jnp.zeros((8, COLS), F32)
        for c in range(PER_GROUP):
            s = slice(8 * c, 8 * c + 8)
            left_sum += left_col[s] * rp[b, s]
            right_sum += right_col[s] * jnp.where(lane8 == 0, right_right[s], rc[b, s])
        el[b] = left_sum
        er[b] = right_sum * flag(right_ok)

    scale = [flag(row_ok[r]) * (1.0 / PER_GROUP) for r in (-1, 0, 1)]

    def correlate(rows):
        def pair(k, carry):
            for b in rows:
                found = ([], [], [])
                for u in range(2):
                    d = 2 * k - 1 + u
                    turn = jnp.maximum(d, 0)
                    factor = jnp.where((d >= 0) & (d < DISPS), scale[b], 0.0)
                    keep = lane8 < COLS - turn
                    total = jnp.zeros((8, COLS), F32)
                    for c in range(PER_GROUP):
                        s = slice(8 * c, 8 * c + 8)
                        mixed = jnp.where(keep, rc[b, s], rp[b, s])
                        total += pltpu.roll(mixed, turn, 1) * lp[b, s]
                    raw = total * factor
                    left = pltpu.roll(el[b], turn, 1) * factor
                    right = pltpu.roll(er[b], turn, 1) * factor
                    found[0].append(pltpu.roll(jnp.where(lane8 == COLS - 1, left, raw), 1, 1))
                    found[1].append(raw)
                    found[2].append(pltpu.roll(jnp.where(lane8 == 0, right, raw), COLS - 1, 1))
                at = pl.multiple_of(16 * k, 16)
                for e in range(3):
                    ins[b, e, pl.ds(at, 16), :] = jnp.concatenate(found[e], 0).astype(BF16)
            return carry

        lax.fori_loop(0, PAIRS, pair, 0)

    for key in [(0, -1, "p"), (0, -1, "e"), (0, 1, "e")]:
        feats[key].wait_recv()
    prepare(1)
    correlate([1])
    for key in feats:
        if key[0] != 0:
            feats[key].wait_recv()
    prepare(0)
    prepare(2)
    correlate([0, 2])

    gain = jnp.zeros((8, COLS), F32)
    for g in range(GROUPS):
        gain = jnp.where(iota((8, COLS), 0) == g, gain_ref[g], gain)
    at_disp = [jnp.broadcast_to(ind[t], (8, COLS)) for t in range(ITERS)]
    looked = [jnp.zeros((8, COLS), F32) for _ in range(ITERS)]
    for j in range(7):
        first = BLOCK * 8 * j
        windows = [ins[b, e, first : first + 128, :] for b in range(3) for e in range(3)]
        conv = dot(tw[0 : BLOCK * 8, :], jnp.concatenate(windows, 0))
        raw = windows[4].astype(F32)[8 : 8 + BLOCK * 8]
        volume = (raw + jnp.maximum(conv, 0.0)).astype(BF16).astype(F32)
        volume = volume.reshape(BLOCK, 8, COLS)
        count = min(BLOCK, DISPS - BLOCK * j)
        lg[BLOCK * j : BLOCK * j + BLOCK, :] = jnp.sum(volume * gain[None], axis=1)
        for q in range(count):
            for t in range(ITERS):
                looked[t] = jnp.where(at_disp[t] == BLOCK * j + q, volume[q], looked[t])

    levels = iota((DISPS, COLS), 0)
    valid = levels < lim[...]
    masked = jnp.where(valid, lg[0:DISPS, :], -1e30)
    weights = jnp.where(valid, jnp.exp(masked - jnp.max(masked, axis=0, keepdims=True)), 0.0)
    moment = jnp.sum(weights * levels.astype(F32), axis=0, keepdims=True)
    disparity = moment / jnp.sum(weights, axis=0, keepdims=True) / 8.0

    high = disparity.astype(BF16).astype(F32)
    middle = (disparity - high).astype(BF16).astype(F32)
    low = disparity - high - middle
    sub8 = iota((8, COLS), 0)
    parts = jnp.zeros((8, COLS), F32)
    for i, part in enumerate((high, middle, low)):
        parts = jnp.where(sub8 == i, part, parts)
    lm[2, 1] = jnp.concatenate(looked + [parts], 0).astype(BF16)
    look_copies = [
        remote(lm.at[2, 1], lm.at[r + 2, c + 1], look_send, look_recv, i, -r, -c)
        for i, (r, c) in enumerate(AROUND)
    ]
    for copy in look_copies:
        copy.start()
    for copy in look_copies:
        copy.wait_recv()

    lane32 = iota((32, COLS), 1)
    place = one_hot(iota((EXT, 256), 0) == iota((EXT, 256), 1))
    take = one_hot((iota((128, 128), 0) >= 56) & (iota((128, 128), 0) < 59))
    for r in range(-2, 3):
        def tile(c, ok):
            return jnp.where(ok, lm[r + 2, c + 1].astype(F32), 0.0)

        left, own, right = (
            tile(-1, row_ok[r] & left_ok), tile(0, row_ok[r]), tile(1, row_ok[r] & right_ok)
        )
        lows, highs = [], []
        for s in (-1, 0, 1):
            lows.append(pltpu.roll(jnp.where(lane32 < 120 + s, own, left), 8 - s, 1))
            highs.append(pltpu.roll(jnp.where(lane32 < 120 + s, right, own), 8 - s, 1))
        zero = jnp.zeros((32, COLS), F32)
        wide = jnp.concatenate(
            [jnp.concatenate(lows + [zero], 0), jnp.concatenate(highs + [zero], 0)], 1
        ).astype(BF16)
        found = dot_nt(place, wide)
        lk3[r + 2] = found
        dd[r + 2, 8 : 8 + EXT, :] = dot(found.astype(BF16), take)

    lane_ext = iota((EXT, 128), 1)
    for t in range(ITERS):
        for copy in hidden_sent[t]:
            copy.wait_recv()
        for r in range(-2, 3):
            i = r + 2
            own = jnp.where(row_ok[r], hr[t, i].astype(F32), 0.0)
            left = jnp.where(row_ok[r] & left_ok, hl[t, i].astype(F32), 0.0)
            right = jnp.where(row_ok[r] & right_ok, hrt[t, i].astype(F32), 0.0)
            hf[i, 16 : 16 + COLS, :] = own
            hf[i, 8:16, :] = left[8:16]
            hf[i, 16 + COLS : 24 + COLS, :] = right[0:8]
            for b in range(3):
                x4[i, :, 128 * b : 128 * b + 128] = hf[i, 7 + b : 7 + b + EXT, :].astype(BF16)
            if t > 0:
                dd[i, 8 : 8 + EXT, :] += dot(x4[i, :, 128:256], head)
            inputs = lk3[i]
            for b in range(3):
                shifted = 0.25 * dd[i, 7 + b : 7 + b + EXT, :]
                inputs = jnp.where(lane_ext == 32 * b + 24, shifted, inputs)
            x4[i, :, 384:512] = inputs.astype(BF16)
        for a in range(3):
            w4[a, 384:512, :] = win[t, a]
        gates = jnp.zeros((3 * EXT, 256), F32)
        for a in range(3):
            gates += dot(x4[a : a + 3].reshape(3 * EXT, 512), w4[a, :, 0:256])
        update = jax.nn.sigmoid(gates[EXT : 2 * EXT, 0:128])
        reset = jax.nn.sigmoid(gates[:, 128:256]).reshape(3, EXT, 128)
        rf[:, 8 : 8 + EXT, :] = reset * hf[1:4, 8 : 8 + EXT, :]
        pre = jnp.zeros((EXT, 128), F32)
        for a in range(3):
            for b in range(3):
                xr[:, 128 * b : 128 * b + 128] = rf[a, 7 + b : 7 + b + EXT, :].astype(BF16)
            xr[:, 384:512] = x4[a + 1, :, 384:512]
            pre += dot(xr[...], w4[a, :, 256:384])
        candidate = jnp.tanh(pre)
        fresh = (1.0 - update) * hf[2, 8 : 8 + EXT, :] + update * candidate
        fresh = fresh[8 : 8 + COLS].astype(BF16)
        disparity += dot_nt(head_row, fresh)[0:1]
        if t < ITERS - 1:
            hr[t + 1, 2] = fresh
            hidden_sent.append(hidden_copies(t + 1))
            for copy in hidden_sent[t + 1]:
                copy.start()
        else:
            hid_out[...] = fresh
    disp_out[...] = disparity

    for copy in list(feats.values()) + look_copies + sum(hidden_sent, []):
        copy.wait_send()


def local(
    feat_left, feat_right, limit, indices, hidden_start,
    vol_kernel, group_gain, hid_kernel, in_kernel, head_weight,
):
    any_spec = pl.BlockSpec(memory_space=pl.ANY)
    vmem = pl.BlockSpec(memory_space=pltpu.VMEM)
    dma = pltpu.SemaphoreType.DMA
    disparity, hidden = pl.pallas_call(
        kernel,
        out_shape=(
            jax.ShapeDtypeStruct((1, COLS), F32),
            jax.ShapeDtypeStruct((COLS, HID), BF16),
        ),
        in_specs=[pl.BlockSpec(memory_space=pltpu.SMEM)] + [any_spec] * 9,
        out_specs=(vmem, vmem),
        scratch_shapes=[
            pltpu.VMEM((3, CH, COLS), BF16),
            pltpu.VMEM((3, CH, COLS), BF16),
            pltpu.VMEM((3, CH, COLS), BF16),
            pltpu.VMEM((16, 128), BF16),
            pltpu.VMEM((3, 16, 128), BF16),
            pltpu.VMEM((3, 16, 128), BF16),
            pltpu.VMEM((1, COLS), jnp.int32),
            pltpu.VMEM((ITERS, 1, COLS), jnp.int32),
            pltpu.VMEM((216, 8), BF16),
            pltpu.VMEM((3, 9, 3, 384), BF16),
            pltpu.VMEM((1, HID), BF16),
            pltpu.VMEM((3, CH, COLS), F32),
            pltpu.VMEM((3, CH, COLS), F32),
            pltpu.VMEM((3, CH, COLS), F32),
            pltpu.VMEM((3, 8, COLS), F32),
            pltpu.VMEM((3, 8, COLS), F32),
            pltpu.VMEM((3, 3, PAIRS * 16, COLS), BF16),
            pltpu.VMEM((128, 9 * 128), BF16),
            pltpu.VMEM((104, COLS), F32),
            pltpu.VMEM((ITERS, 5, COLS, HID), BF16),
            pltpu.VMEM((ITERS, 5, 16, HID), BF16),
            pltpu.VMEM((ITERS, 5, 16, HID), BF16),
            pltpu.VMEM((5, 3, 32, COLS), BF16),
            pltpu.VMEM((5, EXT + 16, 128), F32),
            pltpu.VMEM((3, EXT + 16, 128), F32),
            pltpu.VMEM((5, EXT + 16, 128), F32),
            pltpu.VMEM((5, EXT, 128), F32),
            pltpu.VMEM((5, EXT, 512), BF16),
            pltpu.VMEM((EXT, 512), BF16),
            pltpu.VMEM((3, 512, 384), BF16),
            pltpu.VMEM((ITERS, 3, 128, 384), BF16),
            pltpu.VMEM((3, 32, 384), F32),
            dma((9,)),
            dma((13,)),
            dma((13,)),
            dma((ITERS, len(AROUND))),
            dma((ITERS, len(AROUND))),
            dma((len(AROUND),)),
            dma((len(AROUND),)),
        ],
        compiler_params=pltpu.CompilerParams(collective_id=0, has_side_effects=True),
        name="stereo",
    )(
        group_gain,
        feat_left[0],
        feat_right[0],
        limit,
        indices,
        hidden_start[0],
        vol_kernel.reshape(216, 8),
        hid_kernel.reshape(3, 384, 384),
        in_kernel.transpose(0, 2, 1, 3),
        head_weight.reshape(1, HID),
    )
    return disparity, hidden[None]


def solution(mesh):
    in_specs = (
        P("band", None, "disp"),
        P("band", None, "disp"),
        P("band", "disp"),
        P(None, "band", "disp"),
        P("band", "disp", None),
        P(),
        P(),
        P(),
        P(),
        P(),
    )
    out_specs = (P("band", "disp"), P("band", "disp", None))
    return jax.shard_map(local, mesh=mesh, in_specs=in_specs, out_specs=out_specs, check_vma=False)
```

```python
import jax
import jax.numpy as jnp
from jax import lax
from jax.experimental import pallas as pl
from jax.experimental.pallas import tpu as pltpu
from jax.sharding import PartitionSpec as P

GROUPS = 8
DISPS = 96
PER_GROUP = 12
CH = 96
HID = 128
ITERS = 3
COLS = 128

MESH = pl.DeviceIdType.MESH
F32 = jnp.float32
BF16 = jnp.bfloat16

AROUND = [(r, c) for r in range(-2, 3) for c in (-1, 0, 1) if (r, c) != (0, 0)]
BLOCK = 16
WINDOW = 8 * (BLOCK + 2)
EXT = COLS + 16
NT = (((1,), (1,)), ((), ()))


def dot(a, b):
    return jnp.dot(a, b, preferred_element_type=F32)


def dot_nt(a, b):
    return lax.dot_general(a, b, NT, preferred_element_type=F32)


def iota(shape, dim):
    return lax.broadcasted_iota(jnp.int32, shape, dim)


def one_hot(cond):
    return jnp.where(cond, 1.0, 0.0).astype(BF16)


def kernel(
    gain_ref, fl_in, fr_in, lim_in, ind_in, h0_in, vk_in, hk_in, ik_in, hw_in,
    disp_out, hid_out,
    fl, fr, fp, edge, edge_l, edge_r, lim, ind, vk, ik, hw,
    l3, rt, rg, mean, ins, toep, tw, lg,
    hr, hl, hrt, lm, hf, rf, dd, lk3, x4, xr, w4, win, ikf,
    local_sem, feat_send, feat_recv, hid_send, hid_recv, look_send, look_recv,
):
    band, disp = lax.axis_index("band"), lax.axis_index("disp")
    bands, disps = lax.axis_size("band"), lax.axis_size("disp")

    def device(r, c):
        return (lax.rem(band + r + bands, bands), lax.rem(disp + c + disps, disps))

    locals_ = [
        pltpu.make_async_copy(src, dst, local_sem.at[i])
        for i, (src, dst) in enumerate(
            [
                (fl_in, fl.at[1]),
                (fr_in, fr.at[1]),
                (vk_in, vk),
                (ik_in, ik),
                (hw_in, hw),
                (lim_in, lim),
                (ind_in, ind),
                (h0_in, hr.at[0, 2]),
                (hk_in, w4.at[:, 0:384, :]),
            ]
        )
    ]
    for copy in locals_:
        copy.start()

    barrier = pltpu.get_barrier_semaphore()
    for r, c in AROUND:
        pl.semaphore_signal(barrier, inc=1, device_id=device(r, c), device_id_type=MESH)

    locals_[0].wait()
    locals_[1].wait()
    pad = jnp.zeros((32, COLS), BF16)
    row16, lane16 = iota((16, COLS), 0), iota((16, COLS), 1)
    pick_left = one_hot(((row16 == 0) & (lane16 == 0)) | ((row16 == 2) & (lane16 == COLS - 1)))
    pick_right = one_hot((row16 == 1) & (lane16 == 0))
    edge[...] = (
        dot_nt(pick_left, jnp.concatenate([fl[1], pad], 0))
        + dot_nt(pick_right, jnp.concatenate([fr[1], pad], 0))
    ).astype(BF16)

    pl.semaphore_wait(barrier, len(AROUND))

    def remote(src, dst, send, recv, i, r, c):
        return pltpu.make_async_remote_copy(
            src_ref=src, dst_ref=dst, send_sem=send.at[i], recv_sem=recv.at[i],
            device_id=device(r, c), device_id_type=MESH,
        )

    feats = {}
    plan = [(r, -1, "p") for r in (0, -1, 1)] + [(r, -1, "e") for r in (0, -1, 1)]
    plan += [(r, 1, "e") for r in (0, -1, 1)]
    plan += [(r, 0, kind) for r in (-1, 1) for kind in ("l", "r")]
    for i, (r, c, kind) in enumerate(plan):
        src, dst = {
            "p": (fr_in, fp.at[r + 1]),
            "e": (edge, (edge_l if c < 0 else edge_r).at[r + 1]),
            "l": (fl_in, fl.at[r + 1]),
            "r": (fr_in, fr.at[r + 1]),
        }[kind]
        feats[(r, c, kind)] = remote(src, dst, feat_send, feat_recv, i, -r, -c)
        feats[(r, c, kind)].start()

    def hidden_copies(t):
        copies = []
        for i, (r, c) in enumerate(AROUND):
            own = h0_in if t == 0 else hr.at[t, 2]
            if c == 0:
                src, dst = own, hr.at[t, r + 2]
            elif c < 0:
                src, dst = own.at[COLS - 16 : COLS], hl.at[t, r + 2]
            else:
                src, dst = own.at[0:16], hrt.at[t, r + 2]
            copies.append(
                remote(src, dst, hid_send.at[t], hid_recv.at[t], i, -r, -c)
            )
        return copies

    hidden_sent = [hidden_copies(0)]
    for copy in hidden_sent[0]:
        copy.start()

    for copy in locals_[2:]:
        copy.wait()
    lane8 = iota((8, COLS), 1)
    spread = one_hot(iota((8, COLS), 0) == lax.rem(lane8, 8))
    taps = dot(vk[...], spread)
    lane_r = lane8 // 8
    eye = one_hot(iota((128, 128), 0) == iota((128, 128), 1))
    for b in range(3):
        for e in range(3):
            tap = [taps[((a * 3 + b) * 3 + e) * 8 :][:8] for a in range(3)]
            rows = []
            for q in range(BLOCK + 2):
                block = jnp.zeros((8, COLS), F32)
                for a in range(3):
                    block = jnp.where(lane_r == q - 2 + a, tap[a], block)
                rows.append(block)
            at = (b * 3 + e) * WINDOW
            toep[at : at + WINDOW, :] = jnp.concatenate(rows, 0).astype(BF16)
    tw[...] = dot_nt(eye, toep[...]).astype(BF16)

    head_rows = jnp.broadcast_to(hw[...].astype(F32), (128, HID)).astype(BF16)
    head = dot_nt(eye, head_rows).astype(BF16)
    head_row = head_rows[0:16]

    ikf[...] = jnp.zeros_like(ikf)
    for a in range(3):
        for i in range(GROUPS + 1):
            ikf[a, 3 * i : 3 * i + 3, :] = ik[a, i].astype(F32)
    source = iota((128, 32), 1)
    source_i, source_b = source // 3, lax.rem(source, 3)
    for t in range(ITERS):
        goes_to = 32 * source_b + jnp.where(source_i < GROUPS, 8 * t + source_i, 24)
        move = one_hot((source < 27) & (iota((128, 32), 0) == goes_to))
        for a in range(3):
            win[t, a] = dot(move, ikf[a].astype(BF16)).astype(BF16)

    hf[...] = jnp.zeros_like(hf)
    rf[...] = jnp.zeros_like(rf)
    dd[...] = jnp.zeros_like(dd)

    row_ok = {r: (band + r >= 0) & (band + r < bands) for r in range(-2, 3)}
    left_ok, right_ok = disp > 0, disp < disps - 1

    def flag(ok):
        return jnp.where(ok, 1.0, 0.0).astype(F32)

    for delta in range(-1, COLS + 1):
        apart = jnp.bitwise_and(lane8 - delta, COLS - 1)
        at = 8 * (delta + 1)
        mean[at : at + 8, :] = jnp.where(apart < DISPS, 1.0 / PER_GROUP, 0.0)
    in_group = jnp.where(lane8 // PER_GROUP == iota((8, COLS), 0), 1.0, 0.0)
    lane_ch = iota((CH, COLS), 1)
    eye_ch = one_hot(iota((CH, 128), 0) == iota((CH, 128), 1))
    apart_block = iota((128, COLS), 1) - iota((128, COLS), 0) // 8

    def prepare(b):
        def column(ref, row):
            line = ref[b].astype(F32)[row : row + 1]
            return dot_nt(eye_ch, jnp.broadcast_to(line, (128, 128)).astype(BF16))

        there = flag(row_ok[b - 1])
        own = fl[b].astype(F32) * there
        before = column(edge_l, 2) * (there * flag(left_ok))
        after = column(edge_r, 0) * (there * flag(right_ok))
        l3[b, :, 0:128] = jnp.where(lane_ch == 0, before, pltpu.roll(own, 1, 1)).astype(BF16)
        l3[b, :, 128:256] = own.astype(BF16)
        l3[b, :, 256:384] = jnp.where(
            lane_ch == COLS - 1, after, pltpu.roll(own, COLS - 1, 1)
        ).astype(BF16)
        rt[0, 0:COLS, :] = dot_nt(eye, jnp.concatenate([fr[b], pad], 0))
        rt[0, COLS : COLS + 8, :] = edge_r[b].astype(F32)[0:8]
        rt[1, 0:COLS, :] = dot_nt(eye, jnp.concatenate([fp[b], pad], 0)) * flag(left_ok)
        for side in range(2):
            for k in range(COLS // 2):
                rows = [
                    jnp.broadcast_to(rt[side, 2 * k + u : 2 * k + u + 1, :], (8, COLS)) * in_group
                    for u in range(2)
                ]
                rg[side, 16 * k : 16 * k + 16, :] = jnp.concatenate(rows, 0).astype(BF16)
        last = jnp.broadcast_to(rt[0, COLS + 1 : COLS + 2, :], (8, COLS)) * in_group
        rg[0, 8 * COLS : 8 * COLS + 16, :] = jnp.concatenate([last, last], 0).astype(BF16)

    def correlate(b):
        left3 = l3[b]
        beyond = dot(rg[0, 8 * COLS : 8 * COLS + 16, 0:CH], left3[:, 256:384])[0:8]
        tail = [None] * 3
        for blk in range(8):
            rows = slice(128 * blk, 128 * blk + 128)
            own3 = dot(rg[0, rows, 0:CH], left3)
            near3 = dot(rg[1, rows, 0:CH], left3) if blk >= 2 else None
            for e in range(3):
                found = own3[:, 128 * e : 128 * e + 128]
                first = BLOCK * blk - e + 1
                if near3 is not None:
                    found = jnp.where(
                        apart_block >= first, found, near3[:, 128 * e : 128 * e + 128]
                    )
                if blk == 0 and e == 2:
                    found = jnp.concatenate(
                        [jnp.where(lane8 == COLS - 1, beyond, found[0:8]), found[8:]], 0
                    )
                at = 8 * (first + 1)
                found = found * mean[at : at + 128, :]
                if e == 0:
                    ins[b, 0, 128 * blk + 16 : 128 * blk + 144, :] = found.astype(BF16)
                    if blk == 7:
                        ins[b, 0, 0:16, :] = found[112:128].astype(BF16)
                elif e == 2:
                    ins[b, 2, rows, :] = found.astype(BF16)
                    if blk == 0:
                        ins[b, 2, 1024:1040, :] = found[0:16].astype(BF16)
                else:
                    if blk == 0:
                        head8 = found[0:8]
                        ins[b, 1, 16:128, :] = found[8:120].astype(BF16)
                    else:
                        joined = jnp.concatenate([tail, found[0:120]], 0)
                        ins[b, 1, rows, :] = joined.astype(BF16)
                    tail = found[120:128]
        ins[b, 1, 0:16, :] = jnp.concatenate([tail, head8], 0).astype(BF16)
        ins[b, 1, 1024:1040, :] = jnp.concatenate([tail, head8], 0).astype(BF16)

    for key in [(0, -1, "p"), (0, -1, "e"), (0, 1, "e")]:
        feats[key].wait_recv()
    prepare(1)
    correlate(1)
    for key in feats:
        if key[0] != 0:
            feats[key].wait_recv()
    for b in (0, 2):
        prepare(b)
        correlate(b)

    gain = jnp.zeros((8, COLS), F32)
    for g in range(GROUPS):
        gain = jnp.where(iota((8, COLS), 0) == g, gain_ref[g], gain)
    at_rho = [
        jnp.broadcast_to(jnp.bitwise_and(lane8[0:1] - ind[t], COLS - 1), (8, COLS))
        for t in range(ITERS)
    ]
    looked = [jnp.zeros((8, COLS), F32) for _ in range(ITERS)]
    for blk in range(8):
        rows = slice(128 * blk, 128 * blk + WINDOW)
        windows = [ins[b, e, rows, :] for b in range(3) for e in range(3)]
        conv = dot(tw[...], jnp.concatenate(windows, 0))
        raw = windows[4].astype(F32)[8:136]
        volume = (raw + jnp.maximum(conv, 0.0)).astype(BF16).astype(F32)
        volume = volume.reshape(BLOCK, 8, COLS)
        lg[BLOCK * blk : BLOCK * blk + BLOCK, :] = jnp.sum(volume * gain[None], axis=1)
        for q in range(BLOCK):
            for t in range(ITERS):
                looked[t] = jnp.where(at_rho[t] == BLOCK * blk + q, volume[q], looked[t])

    levels = jnp.bitwise_and(iota((COLS, COLS), 1) - iota((COLS, COLS), 0), COLS - 1)
    valid = levels < lim[...]
    masked = jnp.where(valid, lg[...], -1e30)
    weights = jnp.where(valid, jnp.exp(masked - jnp.max(masked, axis=0, keepdims=True)), 0.0)
    moment = jnp.sum(weights * levels.astype(F32), axis=0, keepdims=True)
    disparity = moment / jnp.sum(weights, axis=0, keepdims=True) / 8.0

    high = disparity.astype(BF16).astype(F32)
    middle = (disparity - high).astype(BF16).astype(F32)
    low = disparity - high - middle
    sub8 = iota((8, COLS), 0)
    parts = jnp.zeros((8, COLS), F32)
    for i, part in enumerate((high, middle, low)):
        parts = jnp.where(sub8 == i, part, parts)
    lm[2, 1] = jnp.concatenate(looked + [parts], 0).astype(BF16)
    look_copies = [
        remote(lm.at[2, 1], lm.at[r + 2, c + 1], look_send, look_recv, i, -r, -c)
        for i, (r, c) in enumerate(AROUND)
    ]
    for copy in look_copies:
        copy.start()
    for copy in look_copies:
        copy.wait_recv()

    lane32 = iota((32, COLS), 1)
    place = one_hot(iota((EXT, 256), 0) == iota((EXT, 256), 1))
    take = one_hot((iota((128, 128), 0) >= 56) & (iota((128, 128), 0) < 59))
    for r in range(-2, 3):
        def tile(c, ok):
            return jnp.where(ok, lm[r + 2, c + 1].astype(F32), 0.0)

        left, own, right = (
            tile(-1, row_ok[r] & left_ok), tile(0, row_ok[r]), tile(1, row_ok[r] & right_ok)
        )
        lows, highs = [], []
        for s in (-1, 0, 1):
            lows.append(pltpu.roll(jnp.where(lane32 < 120 + s, own, left), 8 - s, 1))
            highs.append(pltpu.roll(jnp.where(lane32 < 120 + s, right, own), 8 - s, 1))
        zero = jnp.zeros((32, COLS), F32)
        wide = jnp.concatenate(
            [jnp.concatenate(lows + [zero], 0), jnp.concatenate(highs + [zero], 0)], 1
        ).astype(BF16)
        found = dot_nt(place, wide)
        lk3[r + 2] = found
        dd[r + 2, 8 : 8 + EXT, :] = dot(found.astype(BF16), take)

    lane_ext = iota((EXT, 128), 1)
    for t in range(ITERS):
        for copy in hidden_sent[t]:
            copy.wait_recv()
        for r in range(-2, 3):
            i = r + 2
            own = jnp.where(row_ok[r], hr[t, i].astype(F32), 0.0)
            left = jnp.where(row_ok[r] & left_ok, hl[t, i].astype(F32), 0.0)
            right = jnp.where(row_ok[r] & right_ok, hrt[t, i].astype(F32), 0.0)
            hf[i, 16 : 16 + COLS, :] = own
            hf[i, 8:16, :] = left[8:16]
            hf[i, 16 + COLS : 24 + COLS, :] = right[0:8]
            for b in range(3):
                x4[i, :, 128 * b : 128 * b + 128] = hf[i, 7 + b : 7 + b + EXT, :].astype(BF16)
            if t > 0:
                dd[i, 8 : 8 + EXT, :] += dot(x4[i, :, 128:256], head)
            inputs = lk3[i]
            for b in range(3):
                shifted = 0.25 * dd[i, 7 + b : 7 + b + EXT, :]
                inputs = jnp.where(lane_ext == 32 * b + 24, shifted, inputs)
            x4[i, :, 384:512] = inputs.astype(BF16)
        for a in range(3):
            w4[a, 384:512, :] = win[t, a]
        gates = jnp.zeros((3 * EXT, 256), F32)
        for a in range(3):
            gates += dot(x4[a : a + 3].reshape(3 * EXT, 512), w4[a, :, 0:256])
        update = jax.nn.sigmoid(gates[EXT : 2 * EXT, 0:128])
        reset = jax.nn.sigmoid(gates[:, 128:256]).reshape(3, EXT, 128)
        rf[:, 8 : 8 + EXT, :] = reset * hf[1:4, 8 : 8 + EXT, :]
        pre = jnp.zeros((EXT, 128), F32)
        for a in range(3):
            for b in range(3):
                xr[:, 128 * b : 128 * b + 128] = rf[a, 7 + b : 7 + b + EXT, :].astype(BF16)
            xr[:, 384:512] = x4[a + 1, :, 384:512]
            pre += dot(xr[...], w4[a, :, 256:384])
        candidate = jnp.tanh(pre)
        fresh = (1.0 - update) * hf[2, 8 : 8 + EXT, :] + update * candidate
        fresh = fresh[8 : 8 + COLS].astype(BF16)
        disparity += dot_nt(head_row, fresh)[0:1]
        if t < ITERS - 1:
            hr[t + 1, 2] = fresh
            hidden_sent.append(hidden_copies(t + 1))
            for copy in hidden_sent[t + 1]:
                copy.start()
        else:
            hid_out[...] = fresh
    disp_out[...] = disparity

    for copy in list(feats.values()) + look_copies + sum(hidden_sent, []):
        copy.wait_send()


def local(
    feat_left, feat_right, limit, indices, hidden_start,
    vol_kernel, group_gain, hid_kernel, in_kernel, head_weight,
):
    any_spec = pl.BlockSpec(memory_space=pl.ANY)
    vmem = pl.BlockSpec(memory_space=pltpu.VMEM)
    dma = pltpu.SemaphoreType.DMA
    disparity, hidden = pl.pallas_call(
        kernel,
        out_shape=(
            jax.ShapeDtypeStruct((1, COLS), F32),
            jax.ShapeDtypeStruct((COLS, HID), BF16),
        ),
        in_specs=[pl.BlockSpec(memory_space=pltpu.SMEM)] + [any_spec] * 9,
        out_specs=(vmem, vmem),
        scratch_shapes=[
            pltpu.VMEM((3, CH, COLS), BF16),
            pltpu.VMEM((3, CH, COLS), BF16),
            pltpu.VMEM((3, CH, COLS), BF16),
            pltpu.VMEM((16, 128), BF16),
            pltpu.VMEM((3, 16, 128), BF16),
            pltpu.VMEM((3, 16, 128), BF16),
            pltpu.VMEM((1, COLS), jnp.int32),
            pltpu.VMEM((ITERS, 1, COLS), jnp.int32),
            pltpu.VMEM((216, 8), BF16),
            pltpu.VMEM((3, 9, 3, 384), BF16),
            pltpu.VMEM((1, HID), BF16),
            pltpu.VMEM((3, CH, 3 * COLS), BF16),
            pltpu.VMEM((2, COLS + 8, COLS), F32),
            pltpu.VMEM((2, 8 * COLS + 16, COLS), BF16),
            pltpu.VMEM((8 * (COLS + 2), COLS), F32),
            pltpu.VMEM((3, 3, 8 * (COLS + 2), COLS), BF16),
            pltpu.VMEM((9 * WINDOW, COLS), BF16),
            pltpu.VMEM((128, 9 * WINDOW), BF16),
            pltpu.VMEM((COLS, COLS), F32),
            pltpu.VMEM((ITERS, 5, COLS, HID), BF16),
            pltpu.VMEM((ITERS, 5, 16, HID), BF16),
            pltpu.VMEM((ITERS, 5, 16, HID), BF16),
            pltpu.VMEM((5, 3, 32, COLS), BF16),
            pltpu.VMEM((5, EXT + 16, 128), F32),
            pltpu.VMEM((3, EXT + 16, 128), F32),
            pltpu.VMEM((5, EXT + 16, 128), F32),
            pltpu.VMEM((5, EXT, 128), F32),
            pltpu.VMEM((5, EXT, 512), BF16),
            pltpu.VMEM((EXT, 512), BF16),
            pltpu.VMEM((3, 512, 384), BF16),
            pltpu.VMEM((ITERS, 3, 128, 384), BF16),
            pltpu.VMEM((3, 32, 384), F32),
            dma((9,)),
            dma((13,)),
            dma((13,)),
            dma((ITERS, len(AROUND))),
            dma((ITERS, len(AROUND))),
            dma((len(AROUND),)),
            dma((len(AROUND),)),
        ],
        compiler_params=pltpu.CompilerParams(collective_id=0, has_side_effects=True),
        name="stereo",
    )(
        group_gain,
        feat_left[0],
        feat_right[0],
        limit,
        indices,
        hidden_start[0],
        vol_kernel.reshape(216, 8),
        hid_kernel.reshape(3, 384, 384),
        in_kernel.transpose(0, 2, 1, 3),
        head_weight.reshape(1, HID),
    )
    return disparity, hidden[None]


def solution(mesh):
    in_specs = (
        P("band", None, "disp"),
        P("band", None, "disp"),
        P("band", "disp"),
        P(None, "band", "disp"),
        P("band", "disp", None),
        P(),
        P(),
        P(),
        P(),
        P(),
    )
    out_specs = (P("band", "disp"), P("band", "disp", None))
    return jax.shard_map(local, mesh=mesh, in_specs=in_specs, out_specs=out_specs, check_vma=False)
```

```python
import jax
import jax.numpy as jnp
from jax import lax
from jax.experimental import pallas as pl
from jax.experimental.pallas import tpu as pltpu
from jax.sharding import PartitionSpec as P

GROUPS = 8
DISPS = 96
PER_GROUP = 12
CH = 96
HID = 128
ITERS = 3
COLS = 128

MESH = pl.DeviceIdType.MESH
F32 = jnp.float32
BF16 = jnp.bfloat16

REACH = 6
ROWS = 2 * REACH + 1
NEAR = [r for r in range(-REACH, REACH + 1) if r != 0]
BLOCK = 16
WINDOW = 8 * (BLOCK + 2)
EXT = COLS + 16
LOOK_AT = (0, 16, 24)
NT = (((1,), (1,)), ((), ()))


def dot(a, b):
    return jnp.dot(a, b, preferred_element_type=F32)


def dot_nt(a, b):
    return lax.dot_general(a, b, NT, preferred_element_type=F32)


def iota(shape, dim):
    return lax.broadcasted_iota(jnp.int32, shape, dim)


def one_hot(cond):
    return jnp.where(cond, 1.0, 0.0).astype(BF16)


def kernel(
    gain_ref, fl_in, fr_in, lim_in, ind_in, h0_in, vk_in, hk_in, ik_in, hw_in,
    disp_out, hid_out,
    fl, fr, fp, edge, edge_l, edge_r, lim, ind, vk, ik, hw,
    l3, rt, rg, mean, ins, toep, tw, lg,
    hr, hl, hrt, lm, hf, rf, dd, lk3, x4, up, part, w4, win, ikf,
    local_sem, feat_send, feat_recv, hid_send, hid_recv, look_send, look_recv,
):
    band, disp = lax.axis_index("band"), lax.axis_index("disp")
    bands, disps = lax.axis_size("band"), lax.axis_size("disp")

    def device(r, c):
        return (lax.rem(band + r + bands, bands), lax.rem(disp + c + disps, disps))

    locals_ = [
        pltpu.make_async_copy(src, dst, local_sem.at[i])
        for i, (src, dst) in enumerate(
            [
                (fl_in, fl.at[1]),
                (fr_in, fr.at[1]),
                (vk_in, vk),
                (ik_in, ik),
                (hw_in, hw),
                (lim_in, lim),
                (ind_in, ind),
                (h0_in, hr.at[REACH]),
                (hk_in.at[0], w4.at[0:384, :]),
                (hk_in.at[1], w4.at[512:896, :]),
                (hk_in.at[2], w4.at[1024:1408, :]),
            ]
        )
    ]
    for copy in locals_:
        copy.start()

    barrier = pltpu.get_barrier_semaphore()
    row_ok = {r: (band + r >= 0) & (band + r < bands) for r in range(-REACH, REACH + 1)}
    left_ok, right_ok = disp > 0, disp < disps - 1
    expected = jnp.int32(2)
    for c in (-1, 1):
        pl.semaphore_signal(barrier, inc=1, device_id=device(0, c), device_id_type=MESH)
    for r in NEAR:
        expected += jnp.where(row_ok[r], 3, 0)

        @pl.when(row_ok[r])
        def _(r=r):
            for c in (-1, 0, 1):
                pl.semaphore_signal(barrier, inc=1, device_id=device(r, c), device_id_type=MESH)


    locals_[0].wait()
    locals_[1].wait()
    pad = jnp.zeros((32, COLS), BF16)
    row16, lane16 = iota((16, COLS), 0), iota((16, COLS), 1)
    pick_left = one_hot(((row16 == 0) & (lane16 == 0)) | ((row16 == 2) & (lane16 == COLS - 1)))
    pick_right = one_hot((row16 == 1) & (lane16 == 0))
    edge[...] = (
        dot_nt(pick_left, jnp.concatenate([fl[1], pad], 0))
        + dot_nt(pick_right, jnp.concatenate([fr[1], pad], 0))
    ).astype(BF16)

    pl.semaphore_wait(barrier, expected)

    def remote(src, dst, send, recv, i, r, c):
        return pltpu.make_async_remote_copy(
            src_ref=src, dst_ref=dst, send_sem=send.at[i], recv_sem=recv.at[i],
            device_id=device(r, c), device_id_type=MESH,
        )

    def grouped(make):
        groups = {r: [] for r in range(-REACH, REACH + 1)}
        for r, c, copy in make:
            groups[r].append((c, copy))
        return groups

    def start(groups, r):
        if r == 0:
            for _, copy in groups[r]:
                copy.start()
        else:

            @pl.when(row_ok[-r])
            def _():
                for _, copy in groups[r]:
                    copy.start()

    def arrive(groups, r):
        if r == 0:
            for _, copy in groups[r]:
                copy.wait_recv()
        else:

            @pl.when(row_ok[r])
            def _():
                for _, copy in groups[r]:
                    copy.wait_recv()

    def leave(groups, r):
        if r == 0:
            for _, copy in groups[r]:
                copy.wait_send()
        else:

            @pl.when(row_ok[-r])
            def _():
                for _, copy in groups[r]:
                    copy.wait_send()

    feat_make = []
    for r in (0, -1, 1):
        kinds = [(-1, fr_in, fp.at[r + 1]), (-1, edge, edge_l.at[r + 1]), (1, edge, edge_r.at[r + 1])]
        if r != 0:
            kinds += [(0, fl_in, fl.at[r + 1]), (0, fr_in, fr.at[r + 1])]
        for c, src, dst in kinds:
            i = len(feat_make)
            feat_make.append((r, c, remote(src, dst, feat_send, feat_recv, i, -r, -c)))
    feats = grouped(feat_make)
    for r in (0, -1, 1):
        start(feats, r)

    hid_make, look_make = [], []
    for r in range(-REACH, REACH + 1):
        for c in (-1, 0, 1):
            if (r, c) == (0, 0):
                continue
            i, at = len(hid_make), r + REACH
            src, dst = {
                0: (h0_in, hr.at[at]),
                -1: (h0_in.at[COLS - 8 : COLS], hl.at[at]),
                1: (h0_in.at[0:8], hrt.at[at]),
            }[c]
            hid_make.append((r, c, remote(src, dst, hid_send, hid_recv, i, -r, -c)))
            deep = 32 if abs(r) <= 4 else 16
            look_make.append(
                (
                    r,
                    c,
                    remote(
                        lm.at[REACH, 1, 0:deep],
                        lm.at[at, c + 1, 0:deep],
                        look_send,
                        look_recv,
                        i,
                        -r,
                        -c,
                    ),
                )
            )
    hids, looks = grouped(hid_make), grouped(look_make)
    order = [0] + [r * side for r in range(1, REACH + 1) for side in (-1, 1)]

    for copy in locals_[2:]:
        copy.wait()
    lane8 = iota((8, COLS), 1)
    spread = one_hot(iota((8, COLS), 0) == lax.rem(lane8, 8))
    taps = dot(vk[...], spread)
    lane_r = lane8 // 8
    eye = one_hot(iota((128, 128), 0) == iota((128, 128), 1))
    for b in range(3):
        for e in range(3):
            tap = [taps[((a * 3 + b) * 3 + e) * 8 :][:8] for a in range(3)]
            rows = []
            for q in range(BLOCK + 2):
                block = jnp.zeros((8, COLS), F32)
                for a in range(3):
                    block = jnp.where(lane_r == q - 2 + a, tap[a], block)
                rows.append(block)
            at = (b * 3 + e) * WINDOW
            toep[at : at + WINDOW, :] = jnp.concatenate(rows, 0).astype(BF16)
    tw[...] = dot_nt(eye, toep[...]).astype(BF16)

    head_rows = jnp.broadcast_to(hw[...].astype(F32), (128, HID)).astype(BF16)
    head = dot_nt(eye, head_rows).astype(BF16)
    head_row = head_rows[0:16]

    ikf[...] = jnp.zeros_like(ikf)
    for a in range(3):
        for i in range(GROUPS + 1):
            ikf[a, 3 * i : 3 * i + 3, :] = ik[a, i].astype(F32)
    source = iota((128, 32), 1)
    source_i, source_b = source // 3, lax.rem(source, 3)
    for t in range(ITERS):
        goes_to = 32 * source_b + jnp.where(source_i < GROUPS, LOOK_AT[t] + source_i, 8)
        move = one_hot((source < 27) & (iota((128, 32), 0) == goes_to))
        for a in range(3):
            win[t, a] = dot(move, ikf[a].astype(BF16)).astype(BF16)

    hf[...] = jnp.zeros_like(hf)
    rf[...] = jnp.zeros_like(rf)
    dd[...] = jnp.zeros_like(dd)

    def flag(ok):
        return jnp.where(ok, 1.0, 0.0).astype(F32)

    for delta in range(-1, COLS + 1):
        apart = jnp.bitwise_and(lane8 - delta, COLS - 1)
        at = 8 * (delta + 1)
        mean[at : at + 8, :] = jnp.where(apart < DISPS, 1.0 / PER_GROUP, 0.0)
    in_group = jnp.where(lane8 // PER_GROUP == iota((8, COLS), 0), 1.0, 0.0)
    lane_ch = iota((CH, COLS), 1)
    eye_ch = one_hot(iota((CH, 128), 0) == iota((CH, 128), 1))
    apart_block = iota((128, COLS), 1) - iota((128, COLS), 0) // 8

    def prepare(b):
        def column(ref, row):
            line = ref[b].astype(F32)[row : row + 1]
            return dot_nt(eye_ch, jnp.broadcast_to(line, (128, 128)).astype(BF16))

        there = flag(row_ok[b - 1])
        own = fl[b].astype(F32) * there
        before = column(edge_l, 2) * (there * flag(left_ok))
        after = column(edge_r, 0) * (there * flag(right_ok))
        l3[b, :, 0:128] = jnp.where(lane_ch == 0, before, pltpu.roll(own, 1, 1)).astype(BF16)
        l3[b, :, 128:256] = own.astype(BF16)
        l3[b, :, 256:384] = jnp.where(
            lane_ch == COLS - 1, after, pltpu.roll(own, COLS - 1, 1)
        ).astype(BF16)
        rt[0, 0:COLS, :] = dot_nt(eye, jnp.concatenate([fr[b], pad], 0))
        rt[0, COLS : COLS + 8, :] = edge_r[b].astype(F32)[0:8]
        rt[1, 0:COLS, :] = dot_nt(eye, jnp.concatenate([fp[b], pad], 0)) * flag(left_ok)
        for side in range(2):
            for k in range(COLS // 2):
                rows = [
                    jnp.broadcast_to(rt[side, 2 * k + u : 2 * k + u + 1, :], (8, COLS)) * in_group
                    for u in range(2)
                ]
                rg[side, 16 * k : 16 * k + 16, :] = jnp.concatenate(rows, 0).astype(BF16)
        last = jnp.broadcast_to(rt[0, COLS + 1 : COLS + 2, :], (8, COLS)) * in_group
        rg[0, 8 * COLS : 8 * COLS + 16, :] = jnp.concatenate([last, last], 0).astype(BF16)

    def correlate(b):
        left3 = l3[b]
        beyond = dot(rg[0, 8 * COLS : 8 * COLS + 16, 0:CH], left3[:, 256:384])[0:8]
        tail = [None] * 3
        for blk in range(8):
            rows = slice(128 * blk, 128 * blk + 128)
            own3 = dot(rg[0, rows, 0:CH], left3)
            near3 = dot(rg[1, rows, 0:CH], left3) if blk >= 2 else None
            for e in range(3):
                found = own3[:, 128 * e : 128 * e + 128]
                first = BLOCK * blk - e + 1
                if near3 is not None:
                    found = jnp.where(
                        apart_block >= first, found, near3[:, 128 * e : 128 * e + 128]
                    )
                if blk == 0 and e == 2:
                    found = jnp.concatenate(
                        [jnp.where(lane8 == COLS - 1, beyond, found[0:8]), found[8:]], 0
                    )
                at = 8 * (first + 1)
                found = found * mean[at : at + 128, :]
                if e == 0:
                    ins[b, 0, 128 * blk + 16 : 128 * blk + 144, :] = found.astype(BF16)
                    if blk == 7:
                        ins[b, 0, 0:16, :] = found[112:128].astype(BF16)
                elif e == 2:
                    ins[b, 2, rows, :] = found.astype(BF16)
                    if blk == 0:
                        ins[b, 2, 1024:1040, :] = found[0:16].astype(BF16)
                else:
                    if blk == 0:
                        head8 = found[0:8]
                        ins[b, 1, 16:128, :] = found[8:120].astype(BF16)
                    else:
                        joined = jnp.concatenate([tail, found[0:120]], 0)
                        ins[b, 1, rows, :] = joined.astype(BF16)
                    tail = found[120:128]
        ins[b, 1, 0:16, :] = jnp.concatenate([tail, head8], 0).astype(BF16)
        ins[b, 1, 1024:1040, :] = jnp.concatenate([tail, head8], 0).astype(BF16)

    arrive(feats, 0)
    prepare(1)
    correlate(1)
    for r in (-1, 1):
        arrive(feats, r)
    for r in order:
        start(hids, r)
    for b in (0, 2):
        prepare(b)
        correlate(b)

    gain = jnp.zeros((8, COLS), F32)
    for g in range(GROUPS):
        gain = jnp.where(iota((8, COLS), 0) == g, gain_ref[g], gain)
    at_rho = [
        jnp.broadcast_to(jnp.bitwise_and(lane8[0:1] - ind[t], COLS - 1), (8, COLS))
        for t in range(ITERS)
    ]
    looked = [jnp.zeros((8, COLS), F32) for _ in range(ITERS)]
    for blk in range(8):
        rows = slice(128 * blk, 128 * blk + WINDOW)
        windows = [ins[b, e, rows, :] for b in range(3) for e in range(3)]
        conv = dot(tw[...], jnp.concatenate(windows, 0))
        raw = windows[4].astype(F32)[8:136]
        volume = (raw + jnp.maximum(conv, 0.0)).astype(BF16).astype(F32)
        volume = volume.reshape(BLOCK, 8, COLS)
        lg[BLOCK * blk : BLOCK * blk + BLOCK, :] = jnp.sum(volume * gain[None], axis=1)
        for q in range(BLOCK):
            for t in range(ITERS):
                looked[t] = jnp.where(at_rho[t] == BLOCK * blk + q, volume[q], looked[t])

    levels = jnp.bitwise_and(iota((COLS, COLS), 1) - iota((COLS, COLS), 0), COLS - 1)
    valid = levels < lim[...]
    masked = jnp.where(valid, lg[...], -1e30)
    weights = jnp.where(valid, jnp.exp(masked - jnp.max(masked, axis=0, keepdims=True)), 0.0)
    moment = jnp.sum(weights * levels.astype(F32), axis=0, keepdims=True)
    disparity = moment / jnp.sum(weights, axis=0, keepdims=True) / 8.0

    high = disparity.astype(BF16).astype(F32)
    middle = (disparity - high).astype(BF16).astype(F32)
    low = disparity - high - middle
    sub8 = iota((8, COLS), 0)
    parts = jnp.zeros((8, COLS), F32)
    for i, piece in enumerate((high, middle, low)):
        parts = jnp.where(sub8 == i, piece, parts)
    lm[REACH, 1] = jnp.concatenate([looked[0], parts, looked[1], looked[2]], 0).astype(BF16)
    for r in order:
        start(looks, r)

    def side_by_side(ref, i):
        for b in range(3):
            x4[i, :, 128 * b : 128 * b + 128] = ref[i, 7 + b : 7 + b + EXT, :].astype(BF16)

    def taps_of(low, high, lanes):
        return jnp.concatenate(
            [
                x4[low - 1 + a : high - 1 + a, :, lanes].reshape((high - low) * EXT, -1)
                for a in range(3)
            ],
            1,
        )

    def chunks(low, high):
        half = (high - low + 1) // 2 if high - low > 5 else high - low
        return [(k, min(k + half, high)) for k in range(low, high, half)]

    for r in order:
        arrive(hids, r)
    for r in range(-REACH, REACH + 1):
        i = r + REACH
        hf[i, 16 : 16 + COLS, :] = jnp.where(row_ok[r], hr[i].astype(F32), 0.0)
        hf[i, 8:16, :] = jnp.where(row_ok[r] & left_ok, hl[i].astype(F32), 0.0)
        hf[i, 16 + COLS : 24 + COLS, :] = jnp.where(
            row_ok[r] & right_ok, hrt[i].astype(F32), 0.0
        )
        side_by_side(hf, i)
    hid_taps = jnp.concatenate([w4[512 * a : 512 * a + 384, 0:256] for a in range(3)], 0)
    for low, high in chunks(1, ROWS - 1):
        part[low:high] = dot(taps_of(low, high, slice(0, 384)), hid_taps).reshape(
            high - low, EXT, 256
        )
    lane_ext = iota((EXT, 128), 1)
    col = iota((EXT, 128), 0)
    inside = jnp.where(
        (col < 8) & jnp.logical_not(left_ok) | (col >= 8 + COLS) & jnp.logical_not(right_ok), 0.0, 1.0
    )

    for r in order:
        arrive(looks, r)

    lane32 = iota((32, COLS), 1)
    place = one_hot(iota((EXT, 256), 0) == iota((EXT, 256), 1))
    take = one_hot((iota((128, 128), 0) >= 40) & (iota((128, 128), 0) < 43))
    zero = jnp.zeros((32, COLS), F32)
    for r in range(-REACH, REACH + 1):
        i = r + REACH

        def tile(c, ok):
            if abs(r) <= 4:
                return jnp.where(ok, lm[i, c + 1].astype(F32), 0.0)
            return jnp.concatenate(
                [jnp.where(ok, lm[i, c + 1, 0:16].astype(F32), 0.0), zero[0:16]], 0
            )

        left, own, right = (
            tile(-1, row_ok[r] & left_ok), tile(0, row_ok[r]), tile(1, row_ok[r] & right_ok)
        )
        lows, highs = [], []
        for shift in (-1, 0, 1):
            lows.append(pltpu.roll(jnp.where(lane32 < 120 + shift, own, left), 8 - shift, 1))
            highs.append(pltpu.roll(jnp.where(lane32 < 120 + shift, right, own), 8 - shift, 1))
        wide = jnp.concatenate(
            [jnp.concatenate(lows + [zero], 0), jnp.concatenate(highs + [zero], 0)], 1
        ).astype(BF16)
        found = dot_nt(place, wide)
        lk3[i] = found
        dd[i, 8 : 8 + EXT, :] = dot(found.astype(BF16), take)

    for t in range(ITERS):
        reach = REACH - 2 * t
        low, high = REACH - reach, REACH + reach + 1
        for a in range(3):
            w4[512 * a + 384 : 512 * a + 512, :] = win[t, a]
        for i in range(low, high):
            if t > 0:
                side_by_side(hf, i)
                dd[i, 8 : 8 + EXT, :] += dot(x4[i, :, 128:256], head)
            inputs = lk3[i]
            for b in range(3):
                shifted = 0.25 * dd[i, 7 + b : 7 + b + EXT, :]
                inputs = jnp.where(lane_ext == 32 * b + 8, shifted, inputs)
            x4[i, :, 384:512] = inputs.astype(BF16)
        for first, last in chunks(low + 1, high - 1):
            count = last - first
            if t == 0:
                in_taps = jnp.concatenate([win[0, a, :, 0:256] for a in range(3)], 0)
                gates = dot(taps_of(first, last, slice(384, 512)), in_taps)
                gates = gates.reshape(count, EXT, 256) + part[first:last]
            else:
                gates = dot(taps_of(first, last, slice(0, 512)), w4[:, 0:256])
                gates = gates.reshape(count, EXT, 256)
            up[first:last] = jax.nn.sigmoid(gates[:, :, 0:128])
            reset = jax.nn.sigmoid(gates[:, :, 128:256])
            rf[first:last, 8 : 8 + EXT, :] = reset * hf[first:last, 8 : 8 + EXT, :]
        for i in range(low + 1, high - 1):
            side_by_side(rf, i)
        for first, last in chunks(low + 2, high - 2):
            count = last - first
            pre = dot(taps_of(first, last, slice(0, 512)), w4[:, 256:384])
            candidate = jnp.tanh(pre).reshape(count, EXT, 128)
            update = up[first:last]
            fresh = (1.0 - update) * hf[first:last, 8 : 8 + EXT, :] + update * candidate
            if t < ITERS - 1:
                for i in range(first, last):
                    kept = fresh[i - first] * (inside * flag(row_ok[i - REACH]))
                    hf[i, 8 : 8 + EXT, :] = kept.astype(BF16).astype(F32)
            else:
                hf[REACH, 8 : 8 + EXT, :] = fresh[0].astype(BF16).astype(F32)
        own = hf[REACH, 16 : 16 + COLS, :].astype(BF16)
        disparity += dot_nt(head_row, own)[0:1]
    hid_out[...] = own
    disp_out[...] = disparity

    for groups in (feats, hids, looks):
        for r in groups:
            if groups[r]:
                leave(groups, r)


def local(
    feat_left, feat_right, limit, indices, hidden_start,
    vol_kernel, group_gain, hid_kernel, in_kernel, head_weight,
):
    any_spec = pl.BlockSpec(memory_space=pl.ANY)
    vmem = pl.BlockSpec(memory_space=pltpu.VMEM)
    dma = pltpu.SemaphoreType.DMA
    disparity, hidden = pl.pallas_call(
        kernel,
        out_shape=(
            jax.ShapeDtypeStruct((1, COLS), F32),
            jax.ShapeDtypeStruct((COLS, HID), BF16),
        ),
        in_specs=[pl.BlockSpec(memory_space=pltpu.SMEM)] + [any_spec] * 9,
        out_specs=(vmem, vmem),
        scratch_shapes=[
            pltpu.VMEM((3, CH, COLS), BF16),
            pltpu.VMEM((3, CH, COLS), BF16),
            pltpu.VMEM((3, CH, COLS), BF16),
            pltpu.VMEM((16, 128), BF16),
            pltpu.VMEM((3, 16, 128), BF16),
            pltpu.VMEM((3, 16, 128), BF16),
            pltpu.VMEM((1, COLS), jnp.int32),
            pltpu.VMEM((ITERS, 1, COLS), jnp.int32),
            pltpu.VMEM((216, 8), BF16),
            pltpu.VMEM((3, 9, 3, 384), BF16),
            pltpu.VMEM((1, HID), BF16),
            pltpu.VMEM((3, CH, 3 * COLS), BF16),
            pltpu.VMEM((2, COLS + 8, COLS), F32),
            pltpu.VMEM((2, 8 * COLS + 16, COLS), BF16),
            pltpu.VMEM((8 * (COLS + 2), COLS), F32),
            pltpu.VMEM((3, 3, 8 * (COLS + 2), COLS), BF16),
            pltpu.VMEM((9 * WINDOW, COLS), BF16),
            pltpu.VMEM((128, 9 * WINDOW), BF16),
            pltpu.VMEM((COLS, COLS), F32),
            pltpu.VMEM((ROWS, COLS, HID), BF16),
            pltpu.VMEM((ROWS, 8, HID), BF16),
            pltpu.VMEM((ROWS, 8, HID), BF16),
            pltpu.VMEM((ROWS, 3, 32, COLS), BF16),
            pltpu.VMEM((ROWS, EXT + 16, 128), F32),
            pltpu.VMEM((ROWS, EXT + 16, 128), F32),
            pltpu.VMEM((ROWS, EXT + 16, 128), F32),
            pltpu.VMEM((ROWS, EXT, 128), F32),
            pltpu.VMEM((ROWS, EXT, 512), BF16),
            pltpu.VMEM((ROWS, EXT, 128), F32),
            pltpu.VMEM((ROWS, EXT, 256), F32),
            pltpu.VMEM((3 * 512, 384), BF16),
            pltpu.VMEM((ITERS, 3, 128, 384), BF16),
            pltpu.VMEM((3, 32, 384), F32),
            dma((11,)),
            dma((13,)),
            dma((13,)),
            dma((3 * ROWS - 1,)),
            dma((3 * ROWS - 1,)),
            dma((3 * ROWS - 1,)),
            dma((3 * ROWS - 1,)),
        ],
        compiler_params=pltpu.CompilerParams(collective_id=0, has_side_effects=True),
        name="stereo",
    )(
        group_gain,
        feat_left[0],
        feat_right[0],
        limit,
        indices,
        hidden_start[0],
        vol_kernel.reshape(216, 8),
        hid_kernel.reshape(3, 384, 384),
        in_kernel.transpose(0, 2, 1, 3),
        head_weight.reshape(1, HID),
    )
    return disparity, hidden[None]


def solution(mesh):
    in_specs = (
        P("band", None, "disp"),
        P("band", None, "disp"),
        P("band", "disp"),
        P(None, "band", "disp"),
        P("band", "disp", None),
        P(),
        P(),
        P(),
        P(),
        P(),
    )
    out_specs = (P("band", "disp"), P("band", "disp", None))
    return jax.shard_map(local, mesh=mesh, in_specs=in_specs, out_specs=out_specs, check_vma=False)
```

```python
import jax
import jax.numpy as jnp
from jax import lax
from jax.experimental import pallas as pl
from jax.experimental.pallas import tpu as pltpu
from jax.sharding import PartitionSpec as P

GROUPS = 8
DISPS = 96
PER_GROUP = 12
CH = 96
HID = 128
ITERS = 3
COLS = 128

MESH = pl.DeviceIdType.MESH
F32 = jnp.float32
BF16 = jnp.bfloat16

REACH = 6
ROWS = 2 * REACH + 1
NEAR = [r for r in range(-REACH, REACH + 1) if r != 0]
BLOCK = 16
WINDOW = 8 * (BLOCK + 2)
EXT = COLS + 16
LOOK_AT = (0, 16, 24)
NT = (((1,), (1,)), ((), ()))


def dot(a, b):
    return jnp.dot(a, b, preferred_element_type=F32)


def dot_nt(a, b):
    return lax.dot_general(a, b, NT, preferred_element_type=F32)


def iota(shape, dim):
    return lax.broadcasted_iota(jnp.int32, shape, dim)


def one_hot(cond):
    return jnp.where(cond, 1.0, 0.0).astype(BF16)


def kernel(
    gain_ref, fl_in, fr_in, lim_in, ind_in, h0_in, vk_in, hk_in, ik_in, hw_in,
    disp_out, hid_out,
    fl, fr, fp, edge, edge_l, edge_r, lim, ind, vk, ik, hw,
    l3, rt, rg, mean, ins, toep, tw, lg,
    hr, hl, hrt, lm, hf, rf, dd, lk3, x4, up, part, w4, win, ikf,
    local_sem, feat_send, feat_recv, hid_send, hid_recv, look_send, look_recv, known,
):
    band, disp = lax.axis_index("band"), lax.axis_index("disp")
    bands, disps = lax.axis_size("band"), lax.axis_size("disp")

    def device(r, c):
        return (lax.rem(band + r + bands, bands), lax.rem(disp + c + disps, disps))

    locals_ = [
        pltpu.make_async_copy(src, dst, local_sem.at[i])
        for i, (src, dst) in enumerate(
            [
                (fl_in, fl.at[1]),
                (fr_in, fr.at[1]),
                (vk_in, vk),
                (ik_in, ik),
                (hw_in, hw),
                (lim_in, lim),
                (ind_in, ind),
                (h0_in, hr.at[REACH]),
                (hk_in.at[0], w4.at[0:384, :]),
                (hk_in.at[1], w4.at[512:896, :]),
                (hk_in.at[2], w4.at[1024:1408, :]),
            ]
        )
    ]
    for copy in locals_:
        copy.start()

    barrier = pltpu.get_barrier_semaphore()
    row_ok = {r: (band + r >= 0) & (band + r < bands) for r in range(-REACH, REACH + 1)}
    left_ok, right_ok = disp > 0, disp < disps - 1
    col_ok = {-1: left_ok, 0: None, 1: right_ok}

    def there(r, c):
        if r == 0:
            return col_ok[c]
        return row_ok[r] if c == 0 else row_ok[r] & col_ok[c]

    def when(condition, action):
        if condition is None:
            action()
        else:
            pl.when(condition)(action)

    def count(conditions):
        return sum(jnp.where(ok, 1, 0).astype(jnp.int32) for ok in conditions)

    nearest = [(r, c) for r in (-1, 0, 1) for c in (-1, 0, 1) if (r, c) != (0, 0)]
    for r, c in nearest:
        when(
            there(r, c),
            lambda r=r, c=c: pl.semaphore_signal(
                barrier, inc=1, device_id=device(r, c), device_id_type=MESH
            ),
        )

    locals_[0].wait()
    locals_[1].wait()
    pad = jnp.zeros((32, COLS), BF16)
    row16, lane16 = iota((16, COLS), 0), iota((16, COLS), 1)
    pick_left = one_hot(((row16 == 0) & (lane16 == 0)) | ((row16 == 2) & (lane16 == COLS - 1)))
    pick_right = one_hot((row16 == 1) & (lane16 == 0))
    edge[...] = (
        dot_nt(pick_left, jnp.concatenate([fl[1], pad], 0))
        + dot_nt(pick_right, jnp.concatenate([fr[1], pad], 0))
    ).astype(BF16)

    pl.semaphore_wait(barrier, count(there(r, c) for r, c in nearest))

    def tell(step, r):
        for way in (-r, r):
            when(
                there(way, 0),
                lambda way=way: pl.semaphore_signal(
                    known.at[step], inc=1, device_id=device(way, 0), device_id_type=MESH
                ),
            )

    def learn(step, r):
        pl.semaphore_wait(known.at[step], count((there(-r, 0), there(r, 0))))

    tell(0, 1)

    def remote(src, dst, send, recv, i, r, c):
        return pltpu.make_async_remote_copy(
            src_ref=src, dst_ref=dst, send_sem=send.at[i], recv_sem=recv.at[i],
            device_id=device(r, c), device_id_type=MESH,
        )

    def grouped(make):
        groups = {r: [] for r in range(-REACH, REACH + 1)}
        for r, c, copy in make:
            groups[r].append((c, copy))
        return groups

    def each(groups, r, ok_of, action):
        def row():
            for c, copy in groups[r]:
                when(None if c == 0 else ok_of(0, c), lambda copy=copy: action(copy))

        if groups[r]:
            when(ok_of(r, 0), row)

    def start(groups, r):
        each(groups, r, lambda r, c: there(-r, -c), lambda copy: copy.start())

    def arrive(groups, r):
        each(groups, r, there, lambda copy: copy.wait_recv())

    def leave(groups, r):
        each(groups, r, lambda r, c: there(-r, -c), lambda copy: copy.wait_send())

    feat_make = []
    for r in (0, -1, 1):
        kinds = [(-1, fr_in, fp.at[r + 1]), (-1, edge, edge_l.at[r + 1]), (1, edge, edge_r.at[r + 1])]
        if r != 0:
            kinds += [(0, fl_in, fl.at[r + 1]), (0, fr_in, fr.at[r + 1])]
        for c, src, dst in kinds:
            i = len(feat_make)
            feat_make.append((r, c, remote(src, dst, feat_send, feat_recv, i, -r, -c)))
    feats = grouped(feat_make)
    for r in (0, -1, 1):
        start(feats, r)

    hid_make, look_make = [], []
    for r in range(-REACH, REACH + 1):
        for c in (-1, 0, 1):
            if (r, c) == (0, 0):
                continue
            i, at = len(hid_make), r + REACH
            src, dst = {
                0: (h0_in, hr.at[at]),
                -1: (h0_in.at[COLS - 8 : COLS], hl.at[at]),
                1: (h0_in.at[0:8], hrt.at[at]),
            }[c]
            hid_make.append((r, c, remote(src, dst, hid_send, hid_recv, i, -r, -c)))
            deep = 32 if abs(r) <= 4 else 16
            look_make.append(
                (
                    r,
                    c,
                    remote(
                        lm.at[REACH, 1, 0:deep],
                        lm.at[at, c + 1, 0:deep],
                        look_send,
                        look_recv,
                        i,
                        -r,
                        -c,
                    ),
                )
            )
    hids, looks = grouped(hid_make), grouped(look_make)
    order = [0] + [r * side for r in range(1, REACH + 1) for side in (-1, 1)]

    for copy in locals_[2:]:
        copy.wait()
    lane8 = iota((8, COLS), 1)
    spread = one_hot(iota((8, COLS), 0) == lax.rem(lane8, 8))
    taps = dot(vk[...], spread)
    lane_r = lane8 // 8
    eye = one_hot(iota((128, 128), 0) == iota((128, 128), 1))
    for b in range(3):
        for e in range(3):
            tap = [taps[((a * 3 + b) * 3 + e) * 8 :][:8] for a in range(3)]
            rows = []
            for q in range(BLOCK + 2):
                block = jnp.zeros((8, COLS), F32)
                for a in range(3):
                    block = jnp.where(lane_r == q - 2 + a, tap[a], block)
                rows.append(block)
            at = (b * 3 + e) * WINDOW
            toep[at : at + WINDOW, :] = jnp.concatenate(rows, 0).astype(BF16)
    tw[...] = dot_nt(eye, toep[...]).astype(BF16)

    head_rows = jnp.broadcast_to(hw[...].astype(F32), (128, HID)).astype(BF16)
    head = dot_nt(eye, head_rows).astype(BF16)
    head_row = head_rows[0:16]

    ikf[...] = jnp.zeros_like(ikf)
    for a in range(3):
        for i in range(GROUPS + 1):
            ikf[a, 3 * i : 3 * i + 3, :] = ik[a, i].astype(F32)
    source = iota((128, 32), 1)
    source_i, source_b = source // 3, lax.rem(source, 3)
    for t in range(ITERS):
        goes_to = 32 * source_b + jnp.where(source_i < GROUPS, LOOK_AT[t] + source_i, 8)
        move = one_hot((source < 27) & (iota((128, 32), 0) == goes_to))
        for a in range(3):
            win[t, a] = dot(move, ikf[a].astype(BF16)).astype(BF16)

    hf[...] = jnp.zeros_like(hf)
    rf[...] = jnp.zeros_like(rf)
    dd[...] = jnp.zeros_like(dd)

    def flag(ok):
        return jnp.where(ok, 1.0, 0.0).astype(F32)

    for delta in range(-1, COLS + 1):
        apart = jnp.bitwise_and(lane8 - delta, COLS - 1)
        at = 8 * (delta + 1)
        mean[at : at + 8, :] = jnp.where(apart < DISPS, 1.0 / PER_GROUP, 0.0)
    in_group = jnp.where(lane8 // PER_GROUP == iota((8, COLS), 0), 1.0, 0.0)
    lane_ch = iota((CH, COLS), 1)
    eye_ch = one_hot(iota((CH, 128), 0) == iota((CH, 128), 1))
    apart_block = iota((128, COLS), 1) - iota((128, COLS), 0) // 8

    def prepare(b):
        def column(ref, row):
            line = ref[b].astype(F32)[row : row + 1]
            return dot_nt(eye_ch, jnp.broadcast_to(line, (128, 128)).astype(BF16))

        def kept(ok, value):
            return jnp.where(ok, value.astype(F32), 0.0)

        row, row_left, row_right = (row_ok[b - 1], row_ok[b - 1] & left_ok, row_ok[b - 1] & right_ok)
        own = kept(row, fl[b])
        before = kept(row_left, column(edge_l, 2))
        after = kept(row_right, column(edge_r, 0))
        l3[b, :, 0:128] = jnp.where(lane_ch == 0, before, pltpu.roll(own, 1, 1)).astype(BF16)
        l3[b, :, 128:256] = own.astype(BF16)
        l3[b, :, 256:384] = jnp.where(
            lane_ch == COLS - 1, after, pltpu.roll(own, COLS - 1, 1)
        ).astype(BF16)
        rt[0, 0:COLS, :] = dot_nt(eye, jnp.concatenate([kept(row, fr[b]).astype(BF16), pad], 0))
        rt[0, COLS : COLS + 8, :] = kept(row_right, edge_r[b])[0:8]
        rt[1, 0:COLS, :] = dot_nt(eye, jnp.concatenate([kept(row_left, fp[b]).astype(BF16), pad], 0))
        for side in range(2):
            for k in range(COLS // 2):
                rows = [
                    jnp.broadcast_to(rt[side, 2 * k + u : 2 * k + u + 1, :], (8, COLS)) * in_group
                    for u in range(2)
                ]
                rg[side, 16 * k : 16 * k + 16, :] = jnp.concatenate(rows, 0).astype(BF16)
        last = jnp.broadcast_to(rt[0, COLS + 1 : COLS + 2, :], (8, COLS)) * in_group
        rg[0, 8 * COLS : 8 * COLS + 16, :] = jnp.concatenate([last, last], 0).astype(BF16)

    def correlate(b):
        left3 = l3[b]
        beyond = dot(rg[0, 8 * COLS : 8 * COLS + 16, 0:CH], left3[:, 256:384])[0:8]
        tail = [None] * 3
        for blk in range(8):
            rows = slice(128 * blk, 128 * blk + 128)
            own3 = dot(rg[0, rows, 0:CH], left3)
            near3 = dot(rg[1, rows, 0:CH], left3) if blk >= 2 else None
            for e in range(3):
                found = own3[:, 128 * e : 128 * e + 128]
                first = BLOCK * blk - e + 1
                if near3 is not None:
                    found = jnp.where(
                        apart_block >= first, found, near3[:, 128 * e : 128 * e + 128]
                    )
                if blk == 0 and e == 2:
                    found = jnp.concatenate(
                        [jnp.where(lane8 == COLS - 1, beyond, found[0:8]), found[8:]], 0
                    )
                at = 8 * (first + 1)
                found = found * mean[at : at + 128, :]
                if e == 0:
                    ins[b, 0, 128 * blk + 16 : 128 * blk + 144, :] = found.astype(BF16)
                    if blk == 7:
                        ins[b, 0, 0:16, :] = found[112:128].astype(BF16)
                elif e == 2:
                    ins[b, 2, rows, :] = found.astype(BF16)
                    if blk == 0:
                        ins[b, 2, 1024:1040, :] = found[0:16].astype(BF16)
                else:
                    if blk == 0:
                        head8 = found[0:8]
                        ins[b, 1, 16:128, :] = found[8:120].astype(BF16)
                    else:
                        joined = jnp.concatenate([tail, found[0:120]], 0)
                        ins[b, 1, rows, :] = joined.astype(BF16)
                    tail = found[120:128]
        ins[b, 1, 0:16, :] = jnp.concatenate([tail, head8], 0).astype(BF16)
        ins[b, 1, 1024:1040, :] = jnp.concatenate([tail, head8], 0).astype(BF16)

    learn(0, 1)
    tell(1, 2)
    arrive(feats, 0)
    prepare(1)
    correlate(1)
    for r in (-1, 1):
        arrive(feats, r)
    for r in order[:5]:
        start(hids, r)
    learn(1, 2)
    tell(2, 2)
    for r in order[5:9]:
        start(hids, r)
    prepare(0)
    correlate(0)
    learn(2, 2)
    for r in order[9:]:
        start(hids, r)
    prepare(2)
    correlate(2)

    gain = jnp.zeros((8, COLS), F32)
    for g in range(GROUPS):
        gain = jnp.where(iota((8, COLS), 0) == g, gain_ref[g], gain)
    at_rho = [
        jnp.broadcast_to(jnp.bitwise_and(lane8[0:1] - ind[t], COLS - 1), (8, COLS))
        for t in range(ITERS)
    ]
    looked = [jnp.zeros((8, COLS), F32) for _ in range(ITERS)]
    for blk in range(8):
        rows = slice(128 * blk, 128 * blk + WINDOW)
        windows = [ins[b, e, rows, :] for b in range(3) for e in range(3)]
        conv = dot(tw[...], jnp.concatenate(windows, 0))
        raw = windows[4].astype(F32)[8:136]
        volume = (raw + jnp.maximum(conv, 0.0)).astype(BF16).astype(F32)
        volume = volume.reshape(BLOCK, 8, COLS)
        lg[BLOCK * blk : BLOCK * blk + BLOCK, :] = jnp.sum(volume * gain[None], axis=1)
        for q in range(BLOCK):
            for t in range(ITERS):
                looked[t] = jnp.where(at_rho[t] == BLOCK * blk + q, volume[q], looked[t])

    levels = jnp.bitwise_and(iota((COLS, COLS), 1) - iota((COLS, COLS), 0), COLS - 1)
    valid = levels < lim[...]
    masked = jnp.where(valid, lg[...], -1e30)
    weights = jnp.where(valid, jnp.exp(masked - jnp.max(masked, axis=0, keepdims=True)), 0.0)
    moment = jnp.sum(weights * levels.astype(F32), axis=0, keepdims=True)
    disparity = moment / jnp.sum(weights, axis=0, keepdims=True) / 8.0

    high = disparity.astype(BF16).astype(F32)
    middle = (disparity - high).astype(BF16).astype(F32)
    low = disparity - high - middle
    sub8 = iota((8, COLS), 0)
    parts = jnp.zeros((8, COLS), F32)
    for i, piece in enumerate((high, middle, low)):
        parts = jnp.where(sub8 == i, piece, parts)
    lm[REACH, 1] = jnp.concatenate([looked[0], parts, looked[1], looked[2]], 0).astype(BF16)
    for r in order:
        start(looks, r)

    def side_by_side(ref, i):
        for b in range(3):
            x4[i, :, 128 * b : 128 * b + 128] = ref[i, 7 + b : 7 + b + EXT, :].astype(BF16)

    def taps_of(low, high, lanes):
        return jnp.concatenate(
            [
                x4[low - 1 + a : high - 1 + a, :, lanes].reshape((high - low) * EXT, -1)
                for a in range(3)
            ],
            1,
        )

    def chunks(low, high):
        half = (high - low + 1) // 2 if high - low > 5 else high - low
        return [(k, min(k + half, high)) for k in range(low, high, half)]

    for r in order:
        arrive(hids, r)
    for r in range(-REACH, REACH + 1):
        i = r + REACH
        hf[i, 16 : 16 + COLS, :] = jnp.where(row_ok[r], hr[i].astype(F32), 0.0)
        hf[i, 8:16, :] = jnp.where(row_ok[r] & left_ok, hl[i].astype(F32), 0.0)
        hf[i, 16 + COLS : 24 + COLS, :] = jnp.where(
            row_ok[r] & right_ok, hrt[i].astype(F32), 0.0
        )
        side_by_side(hf, i)
    hid_taps = jnp.concatenate([w4[512 * a : 512 * a + 384, 0:256] for a in range(3)], 0)
    for low, high in chunks(1, ROWS - 1):
        part[low:high] = dot(taps_of(low, high, slice(0, 384)), hid_taps).reshape(
            high - low, EXT, 256
        )
    lane_ext = iota((EXT, 128), 1)
    col = iota((EXT, 128), 0)
    inside = jnp.where(
        (col < 8) & jnp.logical_not(left_ok) | (col >= 8 + COLS) & jnp.logical_not(right_ok), 0.0, 1.0
    )

    lane32 = iota((32, COLS), 1)
    place = one_hot(iota((EXT, 256), 0) == iota((EXT, 256), 1))
    take = one_hot((iota((128, 128), 0) >= 40) & (iota((128, 128), 0) < 43))
    zero = jnp.zeros((32, COLS), F32)

    def inputs_of(i):
        inputs = lk3[i]
        for b in range(3):
            shifted = 0.25 * dd[i, 7 + b : 7 + b + EXT, :]
            inputs = jnp.where(lane_ext == 32 * b + 8, shifted, inputs)
        x4[i, :, 384:512] = inputs.astype(BF16)

    for r in order:
        arrive(looks, r)
        i = r + REACH

        def tile(c, ok):
            if abs(r) <= 4:
                return jnp.where(ok, lm[i, c + 1].astype(F32), 0.0)
            return jnp.concatenate(
                [jnp.where(ok, lm[i, c + 1, 0:16].astype(F32), 0.0), zero[0:16]], 0
            )

        left, own, right = (
            tile(-1, row_ok[r] & left_ok), tile(0, row_ok[r]), tile(1, row_ok[r] & right_ok)
        )
        lows, highs = [], []
        for shift in (-1, 0, 1):
            lows.append(pltpu.roll(jnp.where(lane32 < 120 + shift, own, left), 8 - shift, 1))
            highs.append(pltpu.roll(jnp.where(lane32 < 120 + shift, right, own), 8 - shift, 1))
        wide = jnp.concatenate(
            [jnp.concatenate(lows + [zero], 0), jnp.concatenate(highs + [zero], 0)], 1
        ).astype(BF16)
        found = dot_nt(place, wide)
        lk3[i] = found
        dd[i, 8 : 8 + EXT, :] = dot(found.astype(BF16), take)
        inputs_of(i)

    for t in range(ITERS):
        reach = REACH - 2 * t
        low, high = REACH - reach, REACH + reach + 1
        for a in range(3):
            w4[512 * a + 384 : 512 * a + 512, :] = win[t, a]
        for i in range(low, high) if t > 0 else ():
            side_by_side(hf, i)
            dd[i, 8 : 8 + EXT, :] += dot(x4[i, :, 128:256], head)
            inputs_of(i)
        for first, last in chunks(low + 1, high - 1):
            size = last - first
            if t == 0:
                in_taps = jnp.concatenate([win[0, a, :, 0:256] for a in range(3)], 0)
                gates = dot(taps_of(first, last, slice(384, 512)), in_taps)
                gates = gates.reshape(size, EXT, 256) + part[first:last]
            else:
                gates = dot(taps_of(first, last, slice(0, 512)), w4[:, 0:256])
                gates = gates.reshape(size, EXT, 256)
            up[first:last] = jax.nn.sigmoid(gates[:, :, 0:128])
            reset = jax.nn.sigmoid(gates[:, :, 128:256])
            rf[first:last, 8 : 8 + EXT, :] = reset * hf[first:last, 8 : 8 + EXT, :]
        for i in range(low + 1, high - 1):
            side_by_side(rf, i)
        for first, last in chunks(low + 2, high - 2):
            size = last - first
            pre = dot(taps_of(first, last, slice(0, 512)), w4[:, 256:384])
            candidate = jnp.tanh(pre).reshape(size, EXT, 128)
            update = up[first:last]
            fresh = (1.0 - update) * hf[first:last, 8 : 8 + EXT, :] + update * candidate
            if t < ITERS - 1:
                for i in range(first, last):
                    kept = fresh[i - first] * (inside * flag(row_ok[i - REACH]))
                    hf[i, 8 : 8 + EXT, :] = kept.astype(BF16).astype(F32)
            else:
                hf[REACH, 8 : 8 + EXT, :] = fresh[0].astype(BF16).astype(F32)
        own = hf[REACH, 16 : 16 + COLS, :].astype(BF16)
        disparity += dot_nt(head_row, own)[0:1]
    hid_out[...] = own
    disp_out[...] = disparity

    for groups in (feats, hids, looks):
        for r in groups:
            if groups[r]:
                leave(groups, r)


def local(
    feat_left, feat_right, limit, indices, hidden_start,
    vol_kernel, group_gain, hid_kernel, in_kernel, head_weight,
):
    any_spec = pl.BlockSpec(memory_space=pl.ANY)
    vmem = pl.BlockSpec(memory_space=pltpu.VMEM)
    dma = pltpu.SemaphoreType.DMA
    disparity, hidden = pl.pallas_call(
        kernel,
        out_shape=(
            jax.ShapeDtypeStruct((1, COLS), F32),
            jax.ShapeDtypeStruct((COLS, HID), BF16),
        ),
        in_specs=[pl.BlockSpec(memory_space=pltpu.SMEM)] + [any_spec] * 9,
        out_specs=(vmem, vmem),
        scratch_shapes=[
            pltpu.VMEM((3, CH, COLS), BF16),
            pltpu.VMEM((3, CH, COLS), BF16),
            pltpu.VMEM((3, CH, COLS), BF16),
            pltpu.VMEM((16, 128), BF16),
            pltpu.VMEM((3, 16, 128), BF16),
            pltpu.VMEM((3, 16, 128), BF16),
            pltpu.VMEM((1, COLS), jnp.int32),
            pltpu.VMEM((ITERS, 1, COLS), jnp.int32),
            pltpu.VMEM((216, 8), BF16),
            pltpu.VMEM((3, 9, 3, 384), BF16),
            pltpu.VMEM((1, HID), BF16),
            pltpu.VMEM((3, CH, 3 * COLS), BF16),
            pltpu.VMEM((2, COLS + 8, COLS), F32),
            pltpu.VMEM((2, 8 * COLS + 16, COLS), BF16),
            pltpu.VMEM((8 * (COLS + 2), COLS), F32),
            pltpu.VMEM((3, 3, 8 * (COLS + 2), COLS), BF16),
            pltpu.VMEM((9 * WINDOW, COLS), BF16),
            pltpu.VMEM((128, 9 * WINDOW), BF16),
            pltpu.VMEM((COLS, COLS), F32),
            pltpu.VMEM((ROWS, COLS, HID), BF16),
            pltpu.VMEM((ROWS, 8, HID), BF16),
            pltpu.VMEM((ROWS, 8, HID), BF16),
            pltpu.VMEM((ROWS, 3, 32, COLS), BF16),
            pltpu.VMEM((ROWS, EXT + 16, 128), F32),
            pltpu.VMEM((ROWS, EXT + 16, 128), F32),
            pltpu.VMEM((ROWS, EXT + 16, 128), F32),
            pltpu.VMEM((ROWS, EXT, 128), F32),
            pltpu.VMEM((ROWS, EXT, 512), BF16),
            pltpu.VMEM((ROWS, EXT, 128), F32),
            pltpu.VMEM((ROWS, EXT, 256), F32),
            pltpu.VMEM((3 * 512, 384), BF16),
            pltpu.VMEM((ITERS, 3, 128, 384), BF16),
            pltpu.VMEM((3, 32, 384), F32),
            dma((11,)),
            dma((13,)),
            dma((13,)),
            dma((3 * ROWS - 1,)),
            dma((3 * ROWS - 1,)),
            dma((3 * ROWS - 1,)),
            dma((3 * ROWS - 1,)),
            pltpu.SemaphoreType.REGULAR((3,)),
        ],
        compiler_params=pltpu.CompilerParams(collective_id=0, has_side_effects=True),
        name="stereo",
    )(
        group_gain,
        feat_left[0],
        feat_right[0],
        limit,
        indices,
        hidden_start[0],
        vol_kernel.reshape(216, 8),
        hid_kernel.reshape(3, 384, 384),
        in_kernel.transpose(0, 2, 1, 3),
        head_weight.reshape(1, HID),
    )
    return disparity, hidden[None]


def solution(mesh):
    in_specs = (
        P("band", None, "disp"),
        P("band", None, "disp"),
        P("band", "disp"),
        P(None, "band", "disp"),
        P("band", "disp", None),
        P(),
        P(),
        P(),
        P(),
        P(),
    )
    out_specs = (P("band", "disp"), P("band", "disp", None))
    return jax.shard_map(local, mesh=mesh, in_specs=in_specs, out_specs=out_specs, check_vma=False)
```

```python
import jax
import jax.numpy as jnp
from jax import lax
from jax.experimental import pallas as pl
from jax.experimental.pallas import tpu as pltpu
from jax.sharding import PartitionSpec as P

GROUPS = 8
DISPS = 96
PER_GROUP = 12
CH = 96
HID = 128
ITERS = 3
COLS = 128

MESH = pl.DeviceIdType.MESH
F32 = jnp.float32
BF16 = jnp.bfloat16

REACH = 6
ROWS = 2 * REACH + 1
NEAR = [r for r in range(-REACH, REACH + 1) if r != 0]
BLOCK = 16
WINDOW = 8 * (BLOCK + 2)
EXT = COLS + 16
LOOK_AT = (0, 16, 24)
NT = (((1,), (1,)), ((), ()))


def dot(a, b):
    return jnp.dot(a, b, preferred_element_type=F32)


def dot_nt(a, b):
    return lax.dot_general(a, b, NT, preferred_element_type=F32)


def iota(shape, dim):
    return lax.broadcasted_iota(jnp.int32, shape, dim)


def one_hot(cond):
    return jnp.where(cond, 1.0, 0.0).astype(BF16)


def kernel(
    gain_in, fl_in, fr_in, lim_in, ind_in, h0_in, vk_in, hk_in, ik_in, hw_in,
    disp_out, hid_out,
    fl, fr, fp, edge, edge_l, edge_r, lim, ind, vk, ik, hw,
    l3, rt, rg, mean, ins, toep, tw, lg,
    hr, hl, hrt, lm, hf, rf, dd, lk3, x4, up, part, w4, win, ikf,
    local_sem, feat_send, feat_recv, hid_send, hid_recv, look_send, look_recv, known, fin_h, fin_d, gain_ref,
):
    band, disp = lax.axis_index("band"), lax.axis_index("disp")
    bands, disps = lax.axis_size("band"), lax.axis_size("disp")

    def device(r, c):
        return (lax.rem(band + r + bands, bands), lax.rem(disp + c + disps, disps))

    locals_ = [
        pltpu.make_async_copy(src, dst, local_sem.at[i])
        for i, (src, dst) in enumerate(
            [
                (fl_in, fl.at[1]),
                (fr_in, fr.at[1]),
                (gain_in, gain_ref),
                (vk_in, vk),
                (ik_in, ik),
                (hw_in, hw),
                (lim_in, lim),
                (ind_in, ind),
                (h0_in, hr.at[REACH]),
                (hk_in.at[0], w4.at[0:384, :]),
                (hk_in.at[1], w4.at[512:896, :]),
                (hk_in.at[2], w4.at[1024:1408, :]),
            ]
        )
    ]
    for copy in locals_:
        copy.start()

    barrier = pltpu.get_barrier_semaphore()
    row_ok = {r: (band + r >= 0) & (band + r < bands) for r in range(-REACH, REACH + 1)}
    left_ok, right_ok = disp > 0, disp < disps - 1
    col_ok = {-1: left_ok, 0: None, 1: right_ok}

    def there(r, c):
        if r == 0:
            return col_ok[c]
        return row_ok[r] if c == 0 else row_ok[r] & col_ok[c]

    def when(condition, action):
        if condition is None:
            action()
        else:
            pl.when(condition)(action)

    def count(conditions):
        return sum(jnp.where(ok, 1, 0).astype(jnp.int32) for ok in conditions)

    nearest = [(r, c) for r in (-1, 0, 1) for c in (-1, 0, 1) if (r, c) != (0, 0)]
    for r, c in nearest:
        when(
            there(r, c),
            lambda r=r, c=c: pl.semaphore_signal(
                barrier, inc=1, device_id=device(r, c), device_id_type=MESH
            ),
        )

    locals_[0].wait()
    locals_[1].wait()
    pad = jnp.zeros((32, COLS), BF16)
    row16, lane16 = iota((16, COLS), 0), iota((16, COLS), 1)
    pick_left = one_hot(((row16 == 0) & (lane16 == 0)) | ((row16 == 2) & (lane16 == COLS - 1)))
    pick_right = one_hot((row16 == 1) & (lane16 == 0))
    edge[...] = (
        dot_nt(pick_left, jnp.concatenate([fl[1], pad], 0))
        + dot_nt(pick_right, jnp.concatenate([fr[1], pad], 0))
    ).astype(BF16)

    pl.semaphore_wait(barrier, count(there(r, c) for r, c in nearest))

    def tell(step, r):
        for way in (-r, r):
            when(
                there(way, 0),
                lambda way=way: pl.semaphore_signal(
                    known.at[step], inc=1, device_id=device(way, 0), device_id_type=MESH
                ),
            )

    def learn(step, r):
        pl.semaphore_wait(known.at[step], count((there(-r, 0), there(r, 0))))

    tell(0, 1)

    def remote(src, dst, send, recv, i, r, c):
        return pltpu.make_async_remote_copy(
            src_ref=src, dst_ref=dst, send_sem=send.at[i], recv_sem=recv.at[i],
            device_id=device(r, c), device_id_type=MESH,
        )

    def grouped(make):
        groups = {r: [] for r in range(-REACH, REACH + 1)}
        for r, c, copy in make:
            groups[r].append((c, copy))
        return groups

    def each(groups, r, ok_of, action):
        def row():
            for c, copy in groups[r]:
                when(None if c == 0 else ok_of(0, c), lambda copy=copy: action(copy))

        if groups[r]:
            when(ok_of(r, 0), row)

    def start(groups, r):
        each(groups, r, lambda r, c: there(-r, -c), lambda copy: copy.start())

    def arrive(groups, r):
        each(groups, r, there, lambda copy: copy.wait_recv())

    def leave(groups, r):
        each(groups, r, lambda r, c: there(-r, -c), lambda copy: copy.wait_send())

    feat_make = []
    for r in (0, -1, 1):
        kinds = [(-1, fr_in, fp.at[r + 1]), (-1, edge, edge_l.at[r + 1]), (1, edge, edge_r.at[r + 1])]
        if r != 0:
            kinds += [(0, fl_in, fl.at[r + 1]), (0, fr_in, fr.at[r + 1])]
        for c, src, dst in kinds:
            i = len(feat_make)
            feat_make.append((r, c, remote(src, dst, feat_send, feat_recv, i, -r, -c)))
    feats = grouped(feat_make)
    for r in (0, -1, 1):
        start(feats, r)

    hid_make, look_make = [], []
    for r in range(-REACH, REACH + 1):
        for c in (-1, 0, 1):
            if (r, c) == (0, 0):
                continue
            i, at = len(hid_make), r + REACH
            src, dst = {
                0: (h0_in, hr.at[at]),
                -1: (h0_in.at[COLS - 8 : COLS], hl.at[at]),
                1: (h0_in.at[0:8], hrt.at[at]),
            }[c]
            hid_make.append((r, c, remote(src, dst, hid_send, hid_recv, i, -r, -c)))
            deep = 32 if abs(r) <= 4 else 16
            look_make.append(
                (
                    r,
                    c,
                    remote(
                        lm.at[REACH, 1, 0:deep],
                        lm.at[at, c + 1, 0:deep],
                        look_send,
                        look_recv,
                        i,
                        -r,
                        -c,
                    ),
                )
            )
    hids, looks = grouped(hid_make), grouped(look_make)
    order = [0] + [r * side for r in range(1, REACH + 1) for side in (-1, 1)]

    learn(0, 1)
    tell(1, 2)
    for r in order[:5]:
        start(hids, r)

    for copy in locals_[2:]:
        copy.wait()
    lane8 = iota((8, COLS), 1)
    spread = one_hot(iota((8, COLS), 0) == lax.rem(lane8, 8))
    taps = dot(vk[...], spread)
    lane_r = lane8 // 8
    eye = one_hot(iota((128, 128), 0) == iota((128, 128), 1))
    for b in range(3):
        for e in range(3):
            tap = [taps[((a * 3 + b) * 3 + e) * 8 :][:8] for a in range(3)]
            rows = []
            for q in range(BLOCK + 2):
                block = jnp.zeros((8, COLS), F32)
                for a in range(3):
                    block = jnp.where(lane_r == q - 2 + a, tap[a], block)
                rows.append(block)
            at = (b * 3 + e) * WINDOW
            toep[at : at + WINDOW, :] = jnp.concatenate(rows, 0).astype(BF16)
    tw[...] = dot_nt(eye, toep[...]).astype(BF16)

    learn(1, 2)
    tell(2, 2)
    for r in order[5:9]:
        start(hids, r)

    head_rows = jnp.broadcast_to(hw[...].astype(F32), (128, HID)).astype(BF16)
    head = dot_nt(eye, head_rows).astype(BF16)
    head_row = head_rows[0:16]

    ikf[...] = jnp.zeros_like(ikf)
    for a in range(3):
        for i in range(GROUPS + 1):
            ikf[a, 3 * i : 3 * i + 3, :] = ik[a, i].astype(F32)
    source = iota((128, 32), 1)
    source_i, source_b = source // 3, lax.rem(source, 3)
    for t in range(ITERS):
        goes_to = 32 * source_b + jnp.where(source_i < GROUPS, LOOK_AT[t] + source_i, 8)
        move = one_hot((source < 27) & (iota((128, 32), 0) == goes_to))
        for a in range(3):
            win[t, a] = dot(move, ikf[a].astype(BF16)).astype(BF16)

    hf[...] = jnp.zeros_like(hf)
    rf[...] = jnp.zeros_like(rf)
    dd[...] = jnp.zeros_like(dd)

    def flag(ok):
        return jnp.where(ok, 1.0, 0.0).astype(F32)

    for delta in range(-1, COLS + 1):
        apart = jnp.bitwise_and(lane8 - delta, COLS - 1)
        at = 8 * (delta + 1)
        mean[at : at + 8, :] = jnp.where(apart < DISPS, 1.0 / PER_GROUP, 0.0)
    in_group = jnp.where(lane8 // PER_GROUP == iota((8, COLS), 0), 1.0, 0.0)
    lane_ch = iota((CH, COLS), 1)
    eye_ch = one_hot(iota((CH, 128), 0) == iota((CH, 128), 1))
    apart_block = iota((128, COLS), 1) - iota((128, COLS), 0) // 8

    def prepare(b):
        def column(ref, row):
            line = ref[b].astype(F32)[row : row + 1]
            return dot_nt(eye_ch, jnp.broadcast_to(line, (128, 128)).astype(BF16))

        def kept(ok, value):
            return jnp.where(ok, value.astype(F32), 0.0)

        row, row_left, row_right = (row_ok[b - 1], row_ok[b - 1] & left_ok, row_ok[b - 1] & right_ok)
        own = kept(row, fl[b])
        before = kept(row_left, column(edge_l, 2))
        after = kept(row_right, column(edge_r, 0))
        l3[b, :, 0:128] = jnp.where(lane_ch == 0, before, pltpu.roll(own, 1, 1)).astype(BF16)
        l3[b, :, 128:256] = own.astype(BF16)
        l3[b, :, 256:384] = jnp.where(
            lane_ch == COLS - 1, after, pltpu.roll(own, COLS - 1, 1)
        ).astype(BF16)
        rt[0, 0:COLS, :] = dot_nt(eye, jnp.concatenate([kept(row, fr[b]).astype(BF16), pad], 0))
        rt[0, COLS : COLS + 8, :] = kept(row_right, edge_r[b])[0:8]
        rt[1, 0:COLS, :] = dot_nt(eye, jnp.concatenate([kept(row_left, fp[b]).astype(BF16), pad], 0))
        for side in range(2):
            for k in range(COLS // 2):
                rows = [
                    jnp.broadcast_to(rt[side, 2 * k + u : 2 * k + u + 1, :], (8, COLS)) * in_group
                    for u in range(2)
                ]
                rg[side, 16 * k : 16 * k + 16, :] = jnp.concatenate(rows, 0).astype(BF16)
        last = jnp.broadcast_to(rt[0, COLS + 1 : COLS + 2, :], (8, COLS)) * in_group
        rg[0, 8 * COLS : 8 * COLS + 16, :] = jnp.concatenate([last, last], 0).astype(BF16)

    def correlate(b):
        left3 = l3[b]
        beyond = dot(rg[0, 8 * COLS : 8 * COLS + 16, 0:CH], left3[:, 256:384])[0:8]
        tail = [None] * 3
        for blk in range(8):
            rows = slice(128 * blk, 128 * blk + 128)
            own3 = dot(rg[0, rows, 0:CH], left3)
            near3 = dot(rg[1, rows, 0:CH], left3) if blk >= 2 else None
            for e in range(3):
                found = own3[:, 128 * e : 128 * e + 128]
                first = BLOCK * blk - e + 1
                if near3 is not None:
                    found = jnp.where(
                        apart_block >= first, found, near3[:, 128 * e : 128 * e + 128]
                    )
                if blk == 0 and e == 2:
                    found = jnp.concatenate(
                        [jnp.where(lane8 == COLS - 1, beyond, found[0:8]), found[8:]], 0
                    )
                at = 8 * (first + 1)
                found = found * mean[at : at + 128, :]
                if e == 0:
                    ins[b, 0, 128 * blk + 16 : 128 * blk + 144, :] = found.astype(BF16)
                    if blk == 7:
                        ins[b, 0, 0:16, :] = found[112:128].astype(BF16)
                elif e == 2:
                    ins[b, 2, rows, :] = found.astype(BF16)
                    if blk == 0:
                        ins[b, 2, 1024:1040, :] = found[0:16].astype(BF16)
                else:
                    if blk == 0:
                        head8 = found[0:8]
                        ins[b, 1, 16:128, :] = found[8:120].astype(BF16)
                    else:
                        joined = jnp.concatenate([tail, found[0:120]], 0)
                        ins[b, 1, rows, :] = joined.astype(BF16)
                    tail = found[120:128]
        ins[b, 1, 0:16, :] = jnp.concatenate([tail, head8], 0).astype(BF16)
        ins[b, 1, 1024:1040, :] = jnp.concatenate([tail, head8], 0).astype(BF16)

    learn(2, 2)
    for r in order[9:]:
        start(hids, r)
    arrive(feats, 0)
    prepare(1)
    correlate(1)
    for r in (-1, 1):
        arrive(feats, r)
    for b in (0, 2):
        prepare(b)
        correlate(b)

    gain = jnp.zeros((8, COLS), F32)
    for g in range(GROUPS):
        gain = jnp.where(iota((8, COLS), 0) == g, gain_ref[g], gain)
    at_rho = [
        jnp.broadcast_to(jnp.bitwise_and(lane8[0:1] - ind[t], COLS - 1), (8, COLS))
        for t in range(ITERS)
    ]
    looked = [jnp.zeros((8, COLS), F32) for _ in range(ITERS)]
    for blk in range(8):
        rows = slice(128 * blk, 128 * blk + WINDOW)
        windows = [ins[b, e, rows, :] for b in range(3) for e in range(3)]
        conv = dot(tw[...], jnp.concatenate(windows, 0))
        raw = windows[4].astype(F32)[8:136]
        volume = (raw + jnp.maximum(conv, 0.0)).astype(BF16).astype(F32)
        volume = volume.reshape(BLOCK, 8, COLS)
        lg[BLOCK * blk : BLOCK * blk + BLOCK, :] = jnp.sum(volume * gain[None], axis=1)
        for q in range(BLOCK):
            for t in range(ITERS):
                looked[t] = jnp.where(at_rho[t] == BLOCK * blk + q, volume[q], looked[t])

    levels = jnp.bitwise_and(iota((COLS, COLS), 1) - iota((COLS, COLS), 0), COLS - 1)
    valid = levels < lim[...]
    masked = jnp.where(valid, lg[...], -1e30)
    weights = jnp.where(valid, jnp.exp(masked - jnp.max(masked, axis=0, keepdims=True)), 0.0)
    moment = jnp.sum(weights * levels.astype(F32), axis=0, keepdims=True)
    disparity = moment / jnp.sum(weights, axis=0, keepdims=True) / 8.0

    high = disparity.astype(BF16).astype(F32)
    middle = (disparity - high).astype(BF16).astype(F32)
    low = disparity - high - middle
    sub8 = iota((8, COLS), 0)
    parts = jnp.zeros((8, COLS), F32)
    for i, piece in enumerate((high, middle, low)):
        parts = jnp.where(sub8 == i, piece, parts)
    lm[REACH, 1] = jnp.concatenate([looked[0], parts, looked[1], looked[2]], 0).astype(BF16)
    for r in order:
        start(looks, r)

    def side_by_side(ref, i):
        for b in range(3):
            x4[i, :, 128 * b : 128 * b + 128] = ref[i, 7 + b : 7 + b + EXT, :].astype(BF16)

    def taps_of(low, high, lanes):
        return jnp.concatenate(
            [
                x4[low - 1 + a : high - 1 + a, :, lanes].reshape((high - low) * EXT, -1)
                for a in range(3)
            ],
            1,
        )

    def chunks(low, high):
        half = (high - low + 1) // 2 if high - low > 5 else high - low
        return [(k, min(k + half, high)) for k in range(low, high, half)]

    for r in order:
        arrive(hids, r)
    for r in range(-REACH, REACH + 1):
        i = r + REACH
        hf[i, 16 : 16 + COLS, :] = jnp.where(row_ok[r], hr[i].astype(F32), 0.0)
        hf[i, 8:16, :] = jnp.where(row_ok[r] & left_ok, hl[i].astype(F32), 0.0)
        hf[i, 16 + COLS : 24 + COLS, :] = jnp.where(
            row_ok[r] & right_ok, hrt[i].astype(F32), 0.0
        )
        side_by_side(hf, i)
    hid_taps = jnp.concatenate([w4[512 * a : 512 * a + 384, 0:256] for a in range(3)], 0)
    for low, high in chunks(1, ROWS - 1):
        part[low:high] = dot(taps_of(low, high, slice(0, 384)), hid_taps).reshape(
            high - low, EXT, 256
        )
    lane_ext = iota((EXT, 128), 1)
    col = iota((EXT, 128), 0)
    inside = jnp.where(
        (col < 8) & jnp.logical_not(left_ok) | (col >= 8 + COLS) & jnp.logical_not(right_ok), 0.0, 1.0
    )

    lane32 = iota((32, COLS), 1)
    place = one_hot(iota((EXT, 256), 0) == iota((EXT, 256), 1))
    take = one_hot((iota((128, 128), 0) >= 40) & (iota((128, 128), 0) < 43))
    zero = jnp.zeros((32, COLS), F32)

    def inputs_of(i):
        inputs = lk3[i]
        for b in range(3):
            shifted = 0.25 * dd[i, 7 + b : 7 + b + EXT, :]
            inputs = jnp.where(lane_ext == 32 * b + 8, shifted, inputs)
        x4[i, :, 384:512] = inputs.astype(BF16)

    for r in order:
        arrive(looks, r)
        i = r + REACH

        def tile(c, ok):
            if abs(r) <= 4:
                return jnp.where(ok, lm[i, c + 1].astype(F32), 0.0)
            return jnp.concatenate(
                [jnp.where(ok, lm[i, c + 1, 0:16].astype(F32), 0.0), zero[0:16]], 0
            )

        left, own, right = (
            tile(-1, row_ok[r] & left_ok), tile(0, row_ok[r]), tile(1, row_ok[r] & right_ok)
        )
        lows, highs = [], []
        for shift in (-1, 0, 1):
            lows.append(pltpu.roll(jnp.where(lane32 < 120 + shift, own, left), 8 - shift, 1))
            highs.append(pltpu.roll(jnp.where(lane32 < 120 + shift, right, own), 8 - shift, 1))
        wide = jnp.concatenate(
            [jnp.concatenate(lows + [zero], 0), jnp.concatenate(highs + [zero], 0)], 1
        ).astype(BF16)
        found = dot_nt(place, wide)
        lk3[i] = found
        dd[i, 8 : 8 + EXT, :] = dot(found.astype(BF16), take)
        inputs_of(i)

    for t in range(ITERS):
        reach = REACH - 2 * t
        low, high = REACH - reach, REACH + reach + 1
        for a in range(3):
            w4[512 * a + 384 : 512 * a + 512, :] = win[t, a]
        for i in range(low, high) if t > 0 else ():
            side_by_side(hf, i)
            dd[i, 8 : 8 + EXT, :] += dot(x4[i, :, 128:256], head)
            inputs_of(i)
        for first, last in chunks(low + 1, high - 1):
            size = last - first
            if t == 0:
                in_taps = jnp.concatenate([win[0, a, :, 0:256] for a in range(3)], 0)
                gates = dot(taps_of(first, last, slice(384, 512)), in_taps)
                gates = gates.reshape(size, EXT, 256) + part[first:last]
            else:
                gates = dot(taps_of(first, last, slice(0, 512)), w4[:, 0:256])
                gates = gates.reshape(size, EXT, 256)
            up[first:last] = jax.nn.sigmoid(gates[:, :, 0:128])
            reset = jax.nn.sigmoid(gates[:, :, 128:256])
            rf[first:last, 8 : 8 + EXT, :] = reset * hf[first:last, 8 : 8 + EXT, :]
        for i in range(low + 1, high - 1):
            side_by_side(rf, i)
        for first, last in chunks(low + 2, high - 2):
            size = last - first
            pre = dot(taps_of(first, last, slice(0, 512)), w4[:, 256:384])
            candidate = jnp.tanh(pre).reshape(size, EXT, 128)
            update = up[first:last]
            fresh = (1.0 - update) * hf[first:last, 8 : 8 + EXT, :] + update * candidate
            if t < ITERS - 1:
                for i in range(first, last):
                    kept = fresh[i - first] * (inside * flag(row_ok[i - REACH]))
                    hf[i, 8 : 8 + EXT, :] = kept.astype(BF16).astype(F32)
            else:
                hf[REACH, 8 : 8 + EXT, :] = fresh[0].astype(BF16).astype(F32)
        own = hf[REACH, 16 : 16 + COLS, :].astype(BF16)
        disparity += dot_nt(head_row, own)[0:1]
    fin_h[...] = own
    c1 = pltpu.make_async_copy(fin_h, hid_out, local_sem.at[0])
    c1.start()
    fin_d[...] = disparity
    c2 = pltpu.make_async_copy(fin_d, disp_out, local_sem.at[1])
    c2.start()
    c1.wait()
    c2.wait()

    for groups in (feats, hids, looks):
        for r in groups:
            if groups[r]:
                leave(groups, r)


def local(
    feat_left, feat_right, limit, indices, hidden_start,
    vol_kernel, group_gain, hid_kernel, in_kernel, head_weight,
):
    any_spec = pl.BlockSpec(memory_space=pl.ANY)
    dma = pltpu.SemaphoreType.DMA
    disparity, hidden = pl.pallas_call(
        kernel,
        out_shape=(
            jax.ShapeDtypeStruct((1, COLS), F32),
            jax.ShapeDtypeStruct((COLS, HID), BF16),
        ),
        in_specs=[any_spec] * 10,
        out_specs=(any_spec, any_spec),
        scratch_shapes=[
            pltpu.VMEM((3, CH, COLS), BF16),
            pltpu.VMEM((3, CH, COLS), BF16),
            pltpu.VMEM((3, CH, COLS), BF16),
            pltpu.VMEM((16, 128), BF16),
            pltpu.VMEM((3, 16, 128), BF16),
            pltpu.VMEM((3, 16, 128), BF16),
            pltpu.VMEM((1, COLS), jnp.int32),
            pltpu.VMEM((ITERS, 1, COLS), jnp.int32),
            pltpu.VMEM((216, 8), BF16),
            pltpu.VMEM((3, 9, 3, 384), BF16),
            pltpu.VMEM((1, HID), BF16),
            pltpu.VMEM((3, CH, 3 * COLS), BF16),
            pltpu.VMEM((2, COLS + 8, COLS), F32),
            pltpu.VMEM((2, 8 * COLS + 16, COLS), BF16),
            pltpu.VMEM((8 * (COLS + 2), COLS), F32),
            pltpu.VMEM((3, 3, 8 * (COLS + 2), COLS), BF16),
            pltpu.VMEM((9 * WINDOW, COLS), BF16),
            pltpu.VMEM((128, 9 * WINDOW), BF16),
            pltpu.VMEM((COLS, COLS), F32),
            pltpu.VMEM((ROWS, COLS, HID), BF16),
            pltpu.VMEM((ROWS, 8, HID), BF16),
            pltpu.VMEM((ROWS, 8, HID), BF16),
            pltpu.VMEM((ROWS, 3, 32, COLS), BF16),
            pltpu.VMEM((ROWS, EXT + 16, 128), F32),
            pltpu.VMEM((ROWS, EXT + 16, 128), F32),
            pltpu.VMEM((ROWS, EXT + 16, 128), F32),
            pltpu.VMEM((ROWS, EXT, 128), F32),
            pltpu.VMEM((ROWS, EXT, 512), BF16),
            pltpu.VMEM((ROWS, EXT, 128), F32),
            pltpu.VMEM((ROWS, EXT, 256), F32),
            pltpu.VMEM((3 * 512, 384), BF16),
            pltpu.VMEM((ITERS, 3, 128, 384), BF16),
            pltpu.VMEM((3, 32, 384), F32),
            dma((12,)),
            dma((13,)),
            dma((13,)),
            dma((3 * ROWS - 1,)),
            dma((3 * ROWS - 1,)),
            dma((3 * ROWS - 1,)),
            dma((3 * ROWS - 1,)),
            pltpu.SemaphoreType.REGULAR((3,)),
            pltpu.VMEM((COLS, HID), BF16),
            pltpu.VMEM((1, COLS), F32),
            pltpu.SMEM((GROUPS,), F32),
        ],
        compiler_params=pltpu.CompilerParams(collective_id=0, has_side_effects=True, vmem_limit_bytes=40*2**20),
        name="stereo",
    )(
        *[
            pltpu.with_memory_space_constraint(x, pltpu.HBM)
            for x in (
                group_gain,
                feat_left[0],
                feat_right[0],
                limit,
                indices,
                hidden_start[0],
                vol_kernel.reshape(216, 8),
                hid_kernel.reshape(3, 384, 384),
                in_kernel.transpose(0, 2, 1, 3),
                head_weight.reshape(1, HID),
            )
        ],
    )
    return disparity, hidden[None]


def solution(mesh):
    in_specs = (
        P("band", None, "disp"),
        P("band", None, "disp"),
        P("band", "disp"),
        P(None, "band", "disp"),
        P("band", "disp", None),
        P(),
        P(),
        P(),
        P(),
        P(),
    )
    out_specs = (P("band", "disp"), P("band", "disp", None))
    return jax.shard_map(local, mesh=mesh, in_specs=in_specs, out_specs=out_specs, check_vma=False)
```

```python
import jax
import jax.numpy as jnp
from jax import lax
from jax.experimental import pallas as pl
from jax.experimental.pallas import tpu as pltpu
from jax.sharding import PartitionSpec as P

GROUPS = 8
DISPS = 96
PER_GROUP = 12
CH = 96
HID = 128
ITERS = 3
COLS = 128

MESH = pl.DeviceIdType.MESH
F32 = jnp.float32
BF16 = jnp.bfloat16

REACH = 6
ROWS = 2 * REACH + 1
NEAR = [r for r in range(-REACH, REACH + 1) if r != 0]
BLOCK = 16
WINDOW = 8 * (BLOCK + 2)
EXT = COLS + 16
BOUND = [[BLOCK * blk - e + 1 for e in range(3)] for blk in range(8)]
LOOK_AT = (0, 16, 24)
NT = (((1,), (1,)), ((), ()))


def dot(a, b):
    return jnp.dot(a, b, preferred_element_type=F32)


def dot_nt(a, b):
    return lax.dot_general(a, b, NT, preferred_element_type=F32)


def iota(shape, dim):
    return lax.broadcasted_iota(jnp.int32, shape, dim)


def one_hot(cond):
    return jnp.where(cond, 1.0, 0.0).astype(BF16)


def kernel(
    gain_in, fl_in, fr_in, lim_in, ind_in, h0_in, vk_in, hk_in, ik_in, hw_in,
    disp_out, hid_out,
    fl, fr, fp, edge, edge_l, edge_r, lim, ind, vk, ik, hw,
    l3, rt, rg, mean, ins, toep, tw, lg,
    hr, hl, hrt, lm, hf, rf, dd, lk3, x4, up, part, w4, win, ikf,
    local_sem, feat_send, feat_recv, hid_send, hid_recv, look_send, look_recv, known, fin_h, fin_d, gain_ref,
):
    band, disp = lax.axis_index("band"), lax.axis_index("disp")
    bands, disps = lax.axis_size("band"), lax.axis_size("disp")

    def device(r, c):
        return (lax.rem(band + r + bands, bands), lax.rem(disp + c + disps, disps))

    locals_ = [
        pltpu.make_async_copy(src, dst, local_sem.at[i])
        for i, (src, dst) in enumerate(
            [
                (fl_in, fl.at[1]),
                (fr_in, fr.at[1]),
                (gain_in, gain_ref),
                (vk_in, vk),
                (ik_in, ik),
                (hw_in, hw),
                (lim_in, lim),
                (ind_in, ind),
                (h0_in, hr.at[REACH]),
                (hk_in.at[0], w4.at[0:384, :]),
                (hk_in.at[1], w4.at[512:896, :]),
                (hk_in.at[2], w4.at[1024:1408, :]),
            ]
        )
    ]
    for copy in locals_:
        copy.start()

    barrier = pltpu.get_barrier_semaphore()
    row_ok = {r: (band + r >= 0) & (band + r < bands) for r in range(-REACH, REACH + 1)}
    left_ok, right_ok = disp > 0, disp < disps - 1
    col_ok = {-1: left_ok, 0: None, 1: right_ok}

    def there(r, c):
        if r == 0:
            return col_ok[c]
        return row_ok[r] if c == 0 else row_ok[r] & col_ok[c]

    def when(condition, action):
        if condition is None:
            action()
        else:
            pl.when(condition)(action)

    def count(conditions):
        return sum(jnp.where(ok, 1, 0).astype(jnp.int32) for ok in conditions)

    nearest = [(r, c) for r in (-1, 0, 1) for c in (-1, 0, 1) if (r, c) != (0, 0)]
    for r, c in nearest:
        when(
            there(r, c),
            lambda r=r, c=c: pl.semaphore_signal(
                barrier, inc=1, device_id=device(r, c), device_id_type=MESH
            ),
        )

    locals_[0].wait()
    locals_[1].wait()
    pad = jnp.zeros((32, COLS), BF16)
    row16, lane16 = iota((16, COLS), 0), iota((16, COLS), 1)
    pick_left = one_hot(((row16 == 0) & (lane16 == 0)) | ((row16 == 2) & (lane16 == COLS - 1)))
    pick_right = one_hot((row16 == 1) & (lane16 == 0))
    edge[...] = (
        dot_nt(pick_left, jnp.concatenate([fl[1], pad], 0))
        + dot_nt(pick_right, jnp.concatenate([fr[1], pad], 0))
    ).astype(BF16)

    pl.semaphore_wait(barrier, count(there(r, c) for r, c in nearest))

    def tell(step, r):
        for way in (-r, r):
            when(
                there(way, 0),
                lambda way=way: pl.semaphore_signal(
                    known.at[step], inc=1, device_id=device(way, 0), device_id_type=MESH
                ),
            )

    def learn(step, r):
        pl.semaphore_wait(known.at[step], count((there(-r, 0), there(r, 0))))

    tell(0, 1)

    def remote(src, dst, send, recv, i, r, c):
        return pltpu.make_async_remote_copy(
            src_ref=src, dst_ref=dst, send_sem=send.at[i], recv_sem=recv.at[i],
            device_id=device(r, c), device_id_type=MESH,
        )

    def grouped(make):
        groups = {r: [] for r in range(-REACH, REACH + 1)}
        for r, c, copy in make:
            groups[r].append((c, copy))
        return groups

    def each(groups, r, ok_of, action):
        def row():
            for c, copy in groups[r]:
                when(None if c == 0 else ok_of(0, c), lambda copy=copy: action(copy))

        if groups[r]:
            when(ok_of(r, 0), row)

    def start(groups, r):
        each(groups, r, lambda r, c: there(-r, -c), lambda copy: copy.start())

    def arrive(groups, r):
        each(groups, r, there, lambda copy: copy.wait_recv())

    def leave(groups, r):
        each(groups, r, lambda r, c: there(-r, -c), lambda copy: copy.wait_send())

    feat_make = []
    for r in (0, -1, 1):
        kinds = [(-1, fr_in, fp.at[r + 1]), (-1, edge, edge_l.at[r + 1]), (1, edge, edge_r.at[r + 1])]
        if r != 0:
            kinds += [(0, fl_in, fl.at[r + 1]), (0, fr_in, fr.at[r + 1])]
        for c, src, dst in kinds:
            i = len(feat_make)
            feat_make.append((r, c, remote(src, dst, feat_send, feat_recv, i, -r, -c)))
    feats = grouped(feat_make)
    for r in (0, -1, 1):
        start(feats, r)

    hid_make, look_make = [], []
    for r in range(-REACH, REACH + 1):
        for c in (-1, 0, 1):
            if (r, c) == (0, 0):
                continue
            i, at = len(hid_make), r + REACH
            src, dst = {
                0: (h0_in, hr.at[at]),
                -1: (h0_in.at[COLS - 8 : COLS], hl.at[at]),
                1: (h0_in.at[0:8], hrt.at[at]),
            }[c]
            hid_make.append((r, c, remote(src, dst, hid_send, hid_recv, i, -r, -c)))
            deep = 32 if abs(r) <= 4 else 16
            look_make.append(
                (
                    r,
                    c,
                    remote(
                        lm.at[REACH, 1, 0:deep],
                        lm.at[at, c + 1, 0:deep],
                        look_send,
                        look_recv,
                        i,
                        -r,
                        -c,
                    ),
                )
            )
    hids, looks = grouped(hid_make), grouped(look_make)
    order = [0] + [r * side for r in range(1, REACH + 1) for side in (-1, 1)]

    learn(0, 1)
    tell(1, 2)
    for r in order[:5]:
        start(hids, r)

    for copy in locals_[2:]:
        copy.wait()
    lane8 = iota((8, COLS), 1)
    spread = one_hot(iota((8, COLS), 0) == lax.rem(lane8, 8))
    taps = dot(vk[...], spread)
    lane_r = lane8 // 8
    eye = one_hot(iota((128, 128), 0) == iota((128, 128), 1))
    for b in range(3):
        for e in range(3):
            tap = [taps[((a * 3 + b) * 3 + e) * 8 :][:8] for a in range(3)]
            rows = []
            for q in range(BLOCK + 2):
                block = jnp.zeros((8, COLS), F32)
                for a in range(3):
                    block = jnp.where(lane_r == q - 2 + a, tap[a], block)
                rows.append(block)
            at = (b * 3 + e) * WINDOW
            toep[at : at + WINDOW, :] = jnp.concatenate(rows, 0).astype(BF16)
    tw[...] = dot_nt(eye, toep[...]).astype(BF16)

    learn(1, 2)
    tell(2, 2)
    for r in order[5:9]:
        start(hids, r)

    head_rows = jnp.broadcast_to(hw[...].astype(F32), (128, HID)).astype(BF16)
    head = dot_nt(eye, head_rows).astype(BF16)
    head_row = head_rows[0:16]

    ikf[...] = jnp.zeros_like(ikf)
    for a in range(3):
        for i in range(GROUPS + 1):
            ikf[a, 3 * i : 3 * i + 3, :] = ik[a, i].astype(F32)
    source = iota((128, 32), 1)
    source_i, source_b = source // 3, lax.rem(source, 3)
    for t in range(ITERS):
        goes_to = 32 * source_b + jnp.where(source_i < GROUPS, LOOK_AT[t] + source_i, 8)
        move = one_hot((source < 27) & (iota((128, 32), 0) == goes_to))
        for a in range(3):
            win[t, a] = dot(move, ikf[a].astype(BF16)).astype(BF16)

    hf[...] = jnp.zeros_like(hf)
    rf[...] = jnp.zeros_like(rf)
    dd[...] = jnp.zeros_like(dd)

    def flag(ok):
        return jnp.where(ok, 1.0, 0.0).astype(F32)

    for delta in range(-1, COLS + 1):
        apart = jnp.bitwise_and(lane8 - delta, COLS - 1)
        at = 8 * (delta + 1)
        mean[at : at + 8, :] = jnp.where(apart < DISPS, 1.0 / PER_GROUP, 0.0)
    in_group = jnp.where(lane8 // PER_GROUP == iota((8, COLS), 0), 1.0, 0.0)
    lane_ch = iota((CH, COLS), 1)
    eye_ch = one_hot(iota((CH, 128), 0) == iota((CH, 128), 1))
    pad3 = jnp.zeros((32, 3 * COLS), BF16)

    def prepare(b):
        def column(ref, row):
            line = ref[b].astype(F32)[row : row + 1]
            return dot_nt(eye_ch, jnp.broadcast_to(line, (128, 128)).astype(BF16))

        def kept(ok, value):
            return jnp.where(ok, value.astype(F32), 0.0)

        row, row_left, row_right = (row_ok[b - 1], row_ok[b - 1] & left_ok, row_ok[b - 1] & right_ok)
        own = kept(row, fl[b])
        before = kept(row_left, column(edge_l, 2))
        after = kept(row_right, column(edge_r, 0))
        l3[b, :, 0:128] = jnp.where(lane_ch == 0, before, pltpu.roll(own, 1, 1)).astype(BF16)
        l3[b, :, 128:256] = own.astype(BF16)
        l3[b, :, 256:384] = jnp.where(
            lane_ch == COLS - 1, after, pltpu.roll(own, COLS - 1, 1)
        ).astype(BF16)
        rt[0, 0:COLS, :] = dot_nt(eye, jnp.concatenate([kept(row, fr[b]).astype(BF16), pad], 0))
        rt[0, COLS : COLS + 8, :] = kept(row_right, edge_r[b])[0:8]
        rt[1, 0:COLS, :] = dot_nt(eye, jnp.concatenate([kept(row_left, fp[b]).astype(BF16), pad], 0))
        for side in range(2):
            for k in range(COLS // 2):
                rows = [
                    jnp.broadcast_to(rt[side, 2 * k + u : 2 * k + u + 1, :], (8, COLS)) * in_group
                    for u in range(2)
                ]
                rg[16 * k : 16 * k + 16, 128 * side : 128 * side + 128] = jnp.concatenate(
                    rows, 0
                ).astype(BF16)
        last = jnp.broadcast_to(rt[0, COLS + 1 : COLS + 2, :], (8, COLS)) * in_group
        rg[8 * COLS : 8 * COLS + 16, 0:128] = jnp.concatenate([last, last], 0).astype(BF16)

    def correlate(b):
        left3 = l3[b]
        beyond = dot(rg[8 * COLS : 8 * COLS + 16, 0:CH], left3[:, 256:384])[0:8]
        tail = [None] * 3
        for blk in range(8):
            rows = slice(128 * blk, 128 * blk + 128)
            split = [BOUND[blk][e] for e in range(3)]
            after = one_hot(jnp.concatenate([lane_ch >= at for at in split], 1))
            before = one_hot(jnp.concatenate([lane_ch < at for at in split], 1))
            all3 = dot(rg[rows, :], jnp.concatenate([left3 * after, pad3, left3 * before, pad3], 0))
            for e in range(3):
                found = all3[:, 128 * e : 128 * e + 128]
                first = BLOCK * blk - e + 1
                if blk == 0 and e == 2:
                    found = jnp.concatenate(
                        [jnp.where(lane8 == COLS - 1, beyond, found[0:8]), found[8:]], 0
                    )
                at = 8 * (first + 1)
                found = found * mean[at : at + 128, :]
                if e == 0:
                    ins[b, 0, 128 * blk + 16 : 128 * blk + 144, :] = found.astype(BF16)
                    if blk == 7:
                        ins[b, 0, 0:16, :] = found[112:128].astype(BF16)
                elif e == 2:
                    ins[b, 2, rows, :] = found.astype(BF16)
                    if blk == 0:
                        ins[b, 2, 1024:1040, :] = found[0:16].astype(BF16)
                else:
                    if blk == 0:
                        head8 = found[0:8]
                        ins[b, 1, 16:128, :] = found[8:120].astype(BF16)
                    else:
                        joined = jnp.concatenate([tail, found[0:120]], 0)
                        ins[b, 1, rows, :] = joined.astype(BF16)
                    tail = found[120:128]
        ins[b, 1, 0:16, :] = jnp.concatenate([tail, head8], 0).astype(BF16)
        ins[b, 1, 1024:1040, :] = jnp.concatenate([tail, head8], 0).astype(BF16)

    learn(2, 2)
    for r in order[9:]:
        start(hids, r)
    arrive(feats, 0)
    prepare(1)
    correlate(1)
    for r in (-1, 1):
        arrive(feats, r)
    for b in (0, 2):
        prepare(b)
        correlate(b)

    gain = jnp.zeros((8, COLS), F32)
    for g in range(GROUPS):
        gain = jnp.where(iota((8, COLS), 0) == g, gain_ref[g], gain)
    at_rho = [
        jnp.broadcast_to(jnp.bitwise_and(lane8[0:1] - ind[t], COLS - 1), (8, COLS))
        for t in range(ITERS)
    ]
    looked = [jnp.zeros((8, COLS), F32) for _ in range(ITERS)]
    def window(blk):
        rows = slice(128 * blk, 128 * blk + WINDOW)
        return jnp.concatenate([ins[b, e, rows, :] for b in range(3) for e in range(3)], 0)

    for blk in range(8):
        if blk % 2 == 0:
            both = dot(tw[...], jnp.concatenate([window(blk), window(blk + 1)], 1))
        conv = both[:, 128 * (blk % 2) : 128 * (blk % 2) + 128]
        raw = ins[1, 1, 128 * blk : 128 * blk + WINDOW, :].astype(F32)[8:136]
        volume = (raw + jnp.maximum(conv, 0.0)).astype(BF16).astype(F32)
        volume = volume.reshape(BLOCK, 8, COLS)
        lg[BLOCK * blk : BLOCK * blk + BLOCK, :] = jnp.sum(volume * gain[None], axis=1)
        for q in range(BLOCK):
            for t in range(ITERS):
                looked[t] = jnp.where(at_rho[t] == BLOCK * blk + q, volume[q], looked[t])

    levels = jnp.bitwise_and(iota((COLS, COLS), 1) - iota((COLS, COLS), 0), COLS - 1)
    valid = levels < lim[...]
    masked = jnp.where(valid, lg[...], -1e30)
    weights = jnp.where(valid, jnp.exp(masked - jnp.max(masked, axis=0, keepdims=True)), 0.0)
    moment = jnp.sum(weights * levels.astype(F32), axis=0, keepdims=True)
    disparity = moment / jnp.sum(weights, axis=0, keepdims=True) / 8.0

    high = disparity.astype(BF16).astype(F32)
    middle = (disparity - high).astype(BF16).astype(F32)
    low = disparity - high - middle
    sub8 = iota((8, COLS), 0)
    parts = jnp.zeros((8, COLS), F32)
    for i, piece in enumerate((high, middle, low)):
        parts = jnp.where(sub8 == i, piece, parts)
    lm[REACH, 1] = jnp.concatenate([looked[0], parts, looked[1], looked[2]], 0).astype(BF16)
    for r in reversed(order):
        start(looks, r)

    def side_by_side(ref, i):
        for b in range(3):
            x4[i, :, 128 * b : 128 * b + 128] = ref[i, 7 + b : 7 + b + EXT, :].astype(BF16)

    def taps_of(low, high, lanes):
        return jnp.concatenate(
            [
                x4[low - 1 + a : high - 1 + a, :, lanes].reshape((high - low) * EXT, -1)
                for a in range(3)
            ],
            1,
        )

    def chunks(low, high):
        half = (high - low + 1) // 2 if high - low > 5 else high - low
        return [(k, min(k + half, high)) for k in range(low, high, half)]

    for r in order:
        arrive(hids, r)
    for r in range(-REACH, REACH + 1):
        i = r + REACH
        hf[i, 16 : 16 + COLS, :] = jnp.where(row_ok[r], hr[i].astype(F32), 0.0)
        hf[i, 8:16, :] = jnp.where(row_ok[r] & left_ok, hl[i].astype(F32), 0.0)
        hf[i, 16 + COLS : 24 + COLS, :] = jnp.where(
            row_ok[r] & right_ok, hrt[i].astype(F32), 0.0
        )
        side_by_side(hf, i)
    hid_taps = jnp.concatenate([w4[512 * a : 512 * a + 384, 0:256] for a in range(3)], 0)
    for low, high in chunks(1, ROWS - 1):
        part[low:high] = dot(taps_of(low, high, slice(0, 384)), hid_taps).reshape(
            high - low, EXT, 256
        )
    lane_ext = iota((EXT, 128), 1)
    col = iota((EXT, 128), 0)
    inside = jnp.where(
        (col < 8) & jnp.logical_not(left_ok) | (col >= 8 + COLS) & jnp.logical_not(right_ok), 0.0, 1.0
    )

    lane32 = iota((32, COLS), 1)
    place = one_hot(iota((EXT, 256), 0) == iota((EXT, 256), 1))
    take = one_hot((iota((128, 128), 0) >= 40) & (iota((128, 128), 0) < 43))
    zero = jnp.zeros((32, COLS), F32)

    def inputs_of(i):
        inputs = lk3[i]
        for b in range(3):
            shifted = 0.25 * dd[i, 7 + b : 7 + b + EXT, :]
            inputs = jnp.where(lane_ext == 32 * b + 8, shifted, inputs)
        x4[i, :, 384:512] = inputs.astype(BF16)

    for groups in (feats, hids):
        for r in groups:
            leave(groups, r)
    for at, r in enumerate(order):
        if at in (0, 5, 9):
            for other in order[at : {0: 5, 5: 9, 9: 13}[at]]:
                arrive(looks, other)
        i = r + REACH

        def tile(c, ok):
            if abs(r) <= 4:
                return jnp.where(ok, lm[i, c + 1].astype(F32), 0.0)
            return jnp.concatenate(
                [jnp.where(ok, lm[i, c + 1, 0:16].astype(F32), 0.0), zero[0:16]], 0
            )

        left, own, right = (
            tile(-1, row_ok[r] & left_ok), tile(0, row_ok[r]), tile(1, row_ok[r] & right_ok)
        )
        lows, highs = [], []
        for shift in (-1, 0, 1):
            lows.append(pltpu.roll(jnp.where(lane32 < 120 + shift, own, left), 8 - shift, 1))
            highs.append(pltpu.roll(jnp.where(lane32 < 120 + shift, right, own), 8 - shift, 1))
        wide = jnp.concatenate(
            [jnp.concatenate(lows + [zero], 0), jnp.concatenate(highs + [zero], 0)], 1
        ).astype(BF16)
        found = dot_nt(place, wide)
        lk3[i] = found
        dd[i, 8 : 8 + EXT, :] = dot(found.astype(BF16), take)
        inputs_of(i)

    for r in looks:
        leave(looks, r)

    for t in range(ITERS):
        reach = REACH - 2 * t
        low, high = REACH - reach, REACH + reach + 1
        for a in range(3):
            w4[512 * a + 384 : 512 * a + 512, :] = win[t, a]
        for i in range(low, high) if t > 0 else ():
            side_by_side(hf, i)
            dd[i, 8 : 8 + EXT, :] += dot(x4[i, :, 128:256], head)
            inputs_of(i)
        for first, last in chunks(low + 1, high - 1):
            size = last - first
            if t == 0:
                in_taps = jnp.concatenate([win[0, a, :, 0:256] for a in range(3)], 0)
                gates = dot(taps_of(first, last, slice(384, 512)), in_taps)
                gates = gates.reshape(size, EXT, 256) + part[first:last]
            else:
                gates = dot(taps_of(first, last, slice(0, 512)), w4[:, 0:256])
                gates = gates.reshape(size, EXT, 256)
            up[first:last] = jax.nn.sigmoid(gates[:, :, 0:128])
            reset = jax.nn.sigmoid(gates[:, :, 128:256])
            rf[first:last, 8 : 8 + EXT, :] = reset * hf[first:last, 8 : 8 + EXT, :]
        for i in range(low + 1, high - 1):
            side_by_side(rf, i)
        for first, last in chunks(low + 2, high - 2):
            size = last - first
            pre = dot(taps_of(first, last, slice(0, 512)), w4[:, 256:384])
            candidate = jnp.tanh(pre).reshape(size, EXT, 128)
            update = up[first:last]
            fresh = (1.0 - update) * hf[first:last, 8 : 8 + EXT, :] + update * candidate
            if t < ITERS - 1:
                for i in range(first, last):
                    kept = fresh[i - first] * (inside * flag(row_ok[i - REACH]))
                    hf[i, 8 : 8 + EXT, :] = kept.astype(BF16).astype(F32)
            else:
                hf[REACH, 8 : 8 + EXT, :] = fresh[0].astype(BF16).astype(F32)
        own = hf[REACH, 16 : 16 + COLS, :].astype(BF16)
        disparity += dot_nt(head_row, own)[0:1]
    fin_h[...] = own
    c1 = pltpu.make_async_copy(fin_h, hid_out, local_sem.at[0])
    c1.start()
    fin_d[...] = disparity
    c2 = pltpu.make_async_copy(fin_d, disp_out, local_sem.at[1])
    c2.start()
    c1.wait()
    c2.wait()


def local(
    feat_left, feat_right, limit, indices, hidden_start,
    vol_kernel, group_gain, hid_kernel, in_kernel, head_weight,
):
    any_spec = pl.BlockSpec(memory_space=pl.ANY)
    dma = pltpu.SemaphoreType.DMA
    disparity, hidden = pl.pallas_call(
        kernel,
        out_shape=(
            jax.ShapeDtypeStruct((1, COLS), F32),
            jax.ShapeDtypeStruct((COLS, HID), BF16),
        ),
        in_specs=[any_spec] * 10,
        out_specs=(any_spec, any_spec),
        scratch_shapes=[
            pltpu.VMEM((3, CH, COLS), BF16),
            pltpu.VMEM((3, CH, COLS), BF16),
            pltpu.VMEM((3, CH, COLS), BF16),
            pltpu.VMEM((16, 128), BF16),
            pltpu.VMEM((3, 16, 128), BF16),
            pltpu.VMEM((3, 16, 128), BF16),
            pltpu.VMEM((1, COLS), jnp.int32),
            pltpu.VMEM((ITERS, 1, COLS), jnp.int32),
            pltpu.VMEM((216, 8), BF16),
            pltpu.VMEM((3, 9, 3, 384), BF16),
            pltpu.VMEM((1, HID), BF16),
            pltpu.VMEM((3, CH, 3 * COLS), BF16),
            pltpu.VMEM((2, COLS + 8, COLS), F32),
            pltpu.VMEM((8 * COLS + 16, 2 * COLS), BF16),
            pltpu.VMEM((8 * (COLS + 2), COLS), F32),
            pltpu.VMEM((3, 3, 8 * (COLS + 2), COLS), BF16),
            pltpu.VMEM((9 * WINDOW, COLS), BF16),
            pltpu.VMEM((128, 9 * WINDOW), BF16),
            pltpu.VMEM((COLS, COLS), F32),
            pltpu.VMEM((ROWS, COLS, HID), BF16),
            pltpu.VMEM((ROWS, 8, HID), BF16),
            pltpu.VMEM((ROWS, 8, HID), BF16),
            pltpu.VMEM((ROWS, 3, 32, COLS), BF16),
            pltpu.VMEM((ROWS, EXT + 16, 128), F32),
            pltpu.VMEM((ROWS, EXT + 16, 128), F32),
            pltpu.VMEM((ROWS, EXT + 16, 128), F32),
            pltpu.VMEM((ROWS, EXT, 128), F32),
            pltpu.VMEM((ROWS, EXT, 512), BF16),
            pltpu.VMEM((ROWS, EXT, 128), F32),
            pltpu.VMEM((ROWS, EXT, 256), F32),
            pltpu.VMEM((3 * 512, 384), BF16),
            pltpu.VMEM((ITERS, 3, 128, 384), BF16),
            pltpu.VMEM((3, 32, 384), F32),
            dma((12,)),
            dma((13,)),
            dma((13,)),
            dma((3 * ROWS - 1,)),
            dma((3 * ROWS - 1,)),
            dma((3 * ROWS - 1,)),
            dma((3 * ROWS - 1,)),
            pltpu.SemaphoreType.REGULAR((3,)),
            pltpu.VMEM((COLS, HID), BF16),
            pltpu.VMEM((1, COLS), F32),
            pltpu.SMEM((GROUPS,), F32),
        ],
        compiler_params=pltpu.CompilerParams(collective_id=0, has_side_effects=True, vmem_limit_bytes=40*2**20),
        name="stereo",
    )(
        *[
            pltpu.with_memory_space_constraint(x, pltpu.HBM)
            for x in (
                group_gain,
                feat_left[0],
                feat_right[0],
                limit,
                indices,
                hidden_start[0],
                vol_kernel.reshape(216, 8),
                hid_kernel.reshape(3, 384, 384),
                in_kernel.transpose(0, 2, 1, 3),
                head_weight.reshape(1, HID),
            )
        ],
    )
    return disparity, hidden[None]


def solution(mesh):
    in_specs = (
        P("band", None, "disp"),
        P("band", None, "disp"),
        P("band", "disp"),
        P(None, "band", "disp"),
        P("band", "disp", None),
        P(),
        P(),
        P(),
        P(),
        P(),
    )
    out_specs = (P("band", "disp"), P("band", "disp", None))
    return jax.shard_map(local, mesh=mesh, in_specs=in_specs, out_specs=out_specs, check_vma=False)
```

```python
import jax
import jax.numpy as jnp
from jax import lax
from jax.experimental import pallas as pl
from jax.experimental.pallas import tpu as pltpu
from jax.sharding import PartitionSpec as P

GROUPS = 8
DISPS = 96
PER_GROUP = 12
CH = 96
HID = 128
ITERS = 3
COLS = 128

MESH = pl.DeviceIdType.MESH
F32 = jnp.float32
BF16 = jnp.bfloat16

REACH = 6
ROWS = 2 * REACH + 1
NEAR = [r for r in range(-REACH, REACH + 1) if r != 0]
BLOCK = 16
WINDOW = 8 * (BLOCK + 2)
EXT = COLS + 16
BOUND = [[BLOCK * blk - e + 1 for e in range(3)] for blk in range(8)]
LOOK_AT = (0, 16, 24)
NT = (((1,), (1,)), ((), ()))


def dot(a, b):
    return jnp.dot(a, b, preferred_element_type=F32)


def dot_nt(a, b):
    return lax.dot_general(a, b, NT, preferred_element_type=F32)


def iota(shape, dim):
    return lax.broadcasted_iota(jnp.int32, shape, dim)


def one_hot(cond):
    return jnp.where(cond, 1.0, 0.0).astype(BF16)


def kernel(
    gain_in, fl_in, fr_in, lim_in, ind_in, h0_in, vk_in, hk_in, ik_in, hw_in,
    disp_out, hid_out,
    fl, fr, fp, edge, edge_l, edge_r, lim, ind, vk, ik, hw,
    l3, rt, rg, mean, ins, toep, tw, lg,
    hr, hl, hrt, lm, hf, rf, dd, lk3, x4, up, part, w4, win, ikf,
    local_sem, feat_send, feat_recv, hid_send, hid_recv, look_send, look_recv, known, fin_h, fin_d, gain_ref,
):
    band, disp = lax.axis_index("band"), lax.axis_index("disp")
    bands, disps = lax.axis_size("band"), lax.axis_size("disp")

    def device(r, c):
        return (lax.rem(band + r + bands, bands), lax.rem(disp + c + disps, disps))

    locals_ = [
        pltpu.make_async_copy(src, dst, local_sem.at[i])
        for i, (src, dst) in enumerate(
            [
                (fl_in, fl.at[1]),
                (fr_in, fr.at[1]),
                (gain_in, gain_ref),
                (vk_in, vk),
                (ik_in, ik),
                (hw_in, hw),
                (lim_in, lim),
                (ind_in, ind),
                (h0_in, hr.at[REACH]),
                (hk_in.at[0], w4.at[0:384, :]),
                (hk_in.at[1], w4.at[512:896, :]),
                (hk_in.at[2], w4.at[1024:1408, :]),
            ]
        )
    ]
    for copy in locals_:
        copy.start()

    barrier = pltpu.get_barrier_semaphore()
    row_ok = {r: (band + r >= 0) & (band + r < bands) for r in range(-REACH, REACH + 1)}
    left_ok, right_ok = disp > 0, disp < disps - 1
    col_ok = {-1: left_ok, 0: None, 1: right_ok}

    def there(r, c):
        if r == 0:
            return col_ok[c]
        return row_ok[r] if c == 0 else row_ok[r] & col_ok[c]

    def when(condition, action):
        if condition is None:
            action()
        else:
            pl.when(condition)(action)

    def count(conditions):
        return sum(jnp.where(ok, 1, 0).astype(jnp.int32) for ok in conditions)

    nearest = [(r, c) for r in (-1, 0, 1) for c in (-1, 0, 1) if (r, c) != (0, 0)]
    for r, c in nearest:
        when(
            there(r, c),
            lambda r=r, c=c: pl.semaphore_signal(
                barrier, inc=1, device_id=device(r, c), device_id_type=MESH
            ),
        )

    locals_[0].wait()
    locals_[1].wait()
    pad = jnp.zeros((32, COLS), BF16)
    row16, lane16 = iota((16, COLS), 0), iota((16, COLS), 1)
    pick_left = one_hot(((row16 == 0) & (lane16 == 0)) | ((row16 == 2) & (lane16 == COLS - 1)))
    pick_right = one_hot((row16 == 1) & (lane16 == 0))
    edge[...] = (
        dot_nt(pick_left, jnp.concatenate([fl[1], pad], 0))
        + dot_nt(pick_right, jnp.concatenate([fr[1], pad], 0))
    ).astype(BF16)

    pl.semaphore_wait(barrier, count(there(r, c) for r, c in nearest))

    def tell(step, r):
        for way in (-r, r):
            when(
                there(way, 0),
                lambda way=way: pl.semaphore_signal(
                    known.at[step], inc=1, device_id=device(way, 0), device_id_type=MESH
                ),
            )

    def learn(step, r):
        pl.semaphore_wait(known.at[step], count((there(-r, 0), there(r, 0))))

    tell(0, 1)

    def remote(src, dst, send, recv, i, r, c):
        return pltpu.make_async_remote_copy(
            src_ref=src, dst_ref=dst, send_sem=send.at[i], recv_sem=recv.at[i],
            device_id=device(r, c), device_id_type=MESH,
        )

    def grouped(make):
        groups = {r: [] for r in range(-REACH, REACH + 1)}
        for r, c, copy in make:
            groups[r].append((c, copy))
        return groups

    def each(groups, r, ok_of, action):
        def row():
            for c, copy in groups[r]:
                when(None if c == 0 else ok_of(0, c), lambda copy=copy: action(copy))

        if groups[r]:
            when(ok_of(r, 0), row)

    def start(groups, r):
        each(groups, r, lambda r, c: there(-r, -c), lambda copy: copy.start())

    def arrive(groups, r):
        each(groups, r, there, lambda copy: copy.wait_recv())

    def leave(groups, r):
        each(groups, r, lambda r, c: there(-r, -c), lambda copy: copy.wait_send())

    feat_make = []
    for r in (0, -1, 1):
        kinds = [(-1, fr_in, fp.at[r + 1]), (-1, edge, edge_l.at[r + 1]), (1, edge, edge_r.at[r + 1])]
        if r != 0:
            kinds += [(0, fl_in, fl.at[r + 1]), (0, fr_in, fr.at[r + 1])]
        for c, src, dst in kinds:
            i = len(feat_make)
            feat_make.append((r, c, remote(src, dst, feat_send, feat_recv, i, -r, -c)))
    feats = grouped(feat_make)
    for r in (0, -1, 1):
        start(feats, r)

    hid_make, look_make = [], []
    for r in range(-REACH, REACH + 1):
        for c in (-1, 0, 1):
            if (r, c) == (0, 0):
                continue
            i, at = len(hid_make), r + REACH
            src, dst = {
                0: (h0_in, hr.at[at]),
                -1: (h0_in.at[COLS - 8 : COLS], hl.at[at]),
                1: (h0_in.at[0:8], hrt.at[at]),
            }[c]
            hid_make.append((r, c, remote(src, dst, hid_send, hid_recv, i, -r, -c)))
            deep = 32 if abs(r) <= 4 else 16
            look_make.append(
                (
                    r,
                    c,
                    remote(
                        lm.at[REACH, 1, 0:deep],
                        lm.at[at, c + 1, 0:deep],
                        look_send,
                        look_recv,
                        i,
                        -r,
                        -c,
                    ),
                )
            )
    hids, looks = grouped(hid_make), grouped(look_make)
    order = [0] + [r * side for r in range(1, REACH + 1) for side in (-1, 1)]

    learn(0, 1)
    tell(1, 2)
    for r in order[:5]:
        start(hids, r)

    for copy in locals_[2:]:
        copy.wait()
    lane8 = iota((8, COLS), 1)
    spread = one_hot(iota((8, COLS), 0) == lax.rem(lane8, 8))
    taps = dot(vk[...], spread)
    lane_r = lane8 // 8
    eye = one_hot(iota((128, 128), 0) == iota((128, 128), 1))
    for b in range(3):
        for e in range(3):
            tap = [taps[((a * 3 + b) * 3 + e) * 8 :][:8] for a in range(3)]
            rows = []
            for q in range(BLOCK + 2):
                block = jnp.zeros((8, COLS), F32)
                for a in range(3):
                    block = jnp.where(lane_r == q - 2 + a, tap[a], block)
                rows.append(block)
            at = (b * 3 + e) * WINDOW
            toep[at : at + WINDOW, :] = jnp.concatenate(rows, 0).astype(BF16)
    tw[...] = dot_nt(eye, toep[...]).astype(BF16)

    learn(1, 2)
    tell(2, 2)
    for r in order[5:9]:
        start(hids, r)

    head_rows = jnp.broadcast_to(hw[...].astype(F32), (128, HID)).astype(BF16)
    head = dot_nt(eye, head_rows).astype(BF16)
    head_row = head_rows[0:16]

    ikf[...] = jnp.zeros_like(ikf)
    for a in range(3):
        for i in range(GROUPS + 1):
            ikf[a, 3 * i : 3 * i + 3, :] = ik[a, i].astype(F32)
    source = iota((128, 32), 1)
    source_i, source_b = source // 3, lax.rem(source, 3)
    for t in range(ITERS):
        goes_to = 32 * source_b + jnp.where(source_i < GROUPS, LOOK_AT[t] + source_i, 8)
        move = one_hot((source < 27) & (iota((128, 32), 0) == goes_to))
        for a in range(3):
            win[t, a] = dot(move, ikf[a].astype(BF16)).astype(BF16)

    hf[...] = jnp.zeros_like(hf)
    rf[...] = jnp.zeros_like(rf)
    dd[...] = jnp.zeros_like(dd)

    def flag(ok):
        return jnp.where(ok, 1.0, 0.0).astype(F32)

    for delta in range(-1, COLS + 1):
        apart = jnp.bitwise_and(lane8 - delta, COLS - 1)
        at = 8 * (delta + 1)
        mean[at : at + 8, :] = jnp.where(apart < DISPS, 1.0 / PER_GROUP, 0.0)
    in_group = jnp.where(lane8 // PER_GROUP == iota((8, COLS), 0), 1.0, 0.0)
    lane_ch = iota((CH, COLS), 1)
    eye_ch = one_hot(iota((CH, 128), 0) == iota((CH, 128), 1))
    pad3 = jnp.zeros((32, 3 * COLS), BF16)

    def prepare(b):
        def column(ref, row):
            line = ref[b].astype(F32)[row : row + 1]
            return dot_nt(eye_ch, jnp.broadcast_to(line, (128, 128)).astype(BF16))

        def kept(ok, value):
            return jnp.where(ok, value.astype(F32), 0.0)

        row, row_left, row_right = (row_ok[b - 1], row_ok[b - 1] & left_ok, row_ok[b - 1] & right_ok)
        own = kept(row, fl[b])
        before = kept(row_left, column(edge_l, 2))
        after = kept(row_right, column(edge_r, 0))
        l3[b, :, 0:128] = jnp.where(lane_ch == 0, before, pltpu.roll(own, 1, 1)).astype(BF16)
        l3[b, :, 128:256] = own.astype(BF16)
        l3[b, :, 256:384] = jnp.where(
            lane_ch == COLS - 1, after, pltpu.roll(own, COLS - 1, 1)
        ).astype(BF16)
        rt[0, 0:COLS, :] = dot_nt(eye, jnp.concatenate([kept(row, fr[b]).astype(BF16), pad], 0))
        rt[0, COLS : COLS + 8, :] = kept(row_right, edge_r[b])[0:8]
        rt[1, 0:COLS, :] = dot_nt(eye, jnp.concatenate([kept(row_left, fp[b]).astype(BF16), pad], 0))
        for side in range(2):
            for k in range(COLS // 2):
                rows = [
                    jnp.broadcast_to(rt[side, 2 * k + u : 2 * k + u + 1, :], (8, COLS)) * in_group
                    for u in range(2)
                ]
                rg[16 * k : 16 * k + 16, 128 * side : 128 * side + 128] = jnp.concatenate(
                    rows, 0
                ).astype(BF16)
        last = jnp.broadcast_to(rt[0, COLS + 1 : COLS + 2, :], (8, COLS)) * in_group
        rg[8 * COLS : 8 * COLS + 16, 0:128] = jnp.concatenate([last, last], 0).astype(BF16)

    def correlate(b):
        left3 = l3[b]
        beyond = dot(rg[8 * COLS : 8 * COLS + 16, 0:CH], left3[:, 256:384])[0:8]
        tail = [None] * 3
        for blk in range(8):
            rows = slice(128 * blk, 128 * blk + 128)
            split = [BOUND[blk][e] for e in range(3)]
            after = one_hot(jnp.concatenate([lane_ch >= at for at in split], 1))
            before = one_hot(jnp.concatenate([lane_ch < at for at in split], 1))
            all3 = dot(rg[rows, :], jnp.concatenate([left3 * after, pad3, left3 * before, pad3], 0))
            for e in range(3):
                found = all3[:, 128 * e : 128 * e + 128]
                first = BLOCK * blk - e + 1
                if blk == 0 and e == 2:
                    found = jnp.concatenate(
                        [jnp.where(lane8 == COLS - 1, beyond, found[0:8]), found[8:]], 0
                    )
                at = 8 * (first + 1)
                found = found * mean[at : at + 128, :]
                if e == 0:
                    ins[b, 0, 128 * blk + 16 : 128 * blk + 144, :] = found.astype(BF16)
                    if blk == 7:
                        ins[b, 0, 0:16, :] = found[112:128].astype(BF16)
                elif e == 2:
                    ins[b, 2, rows, :] = found.astype(BF16)
                    if blk == 0:
                        ins[b, 2, 1024:1040, :] = found[0:16].astype(BF16)
                else:
                    if blk == 0:
                        head8 = found[0:8]
                        ins[b, 1, 16:128, :] = found[8:120].astype(BF16)
                    else:
                        joined = jnp.concatenate([tail, found[0:120]], 0)
                        ins[b, 1, rows, :] = joined.astype(BF16)
                    tail = found[120:128]
        ins[b, 1, 0:16, :] = jnp.concatenate([tail, head8], 0).astype(BF16)
        ins[b, 1, 1024:1040, :] = jnp.concatenate([tail, head8], 0).astype(BF16)

    learn(2, 2)
    for r in order[9:]:
        start(hids, r)
    arrive(feats, 0)
    prepare(1)
    correlate(1)
    for b in (0, 2):
        arrive(feats, b - 1)
        prepare(b)
        correlate(b)

    gain = jnp.zeros((8, COLS), F32)
    for g in range(GROUPS):
        gain = jnp.where(iota((8, COLS), 0) == g, gain_ref[g], gain)
    at_rho = [
        jnp.broadcast_to(jnp.bitwise_and(lane8[0:1] - ind[t], COLS - 1), (8, COLS))
        for t in range(ITERS)
    ]
    looked = [jnp.zeros((8, COLS), F32) for _ in range(ITERS)]
    def window(blk):
        rows = slice(128 * blk, 128 * blk + WINDOW)
        return jnp.concatenate([ins[b, e, rows, :] for b in range(3) for e in range(3)], 0)

    for blk in range(8):
        if blk % 2 == 0:
            both = dot(tw[...], jnp.concatenate([window(blk), window(blk + 1)], 1))
        conv = both[:, 128 * (blk % 2) : 128 * (blk % 2) + 128]
        raw = ins[1, 1, 128 * blk : 128 * blk + WINDOW, :].astype(F32)[8:136]
        volume = (raw + jnp.maximum(conv, 0.0)).astype(BF16).astype(F32)
        volume = volume.reshape(BLOCK, 8, COLS)
        lg[BLOCK * blk : BLOCK * blk + BLOCK, :] = jnp.sum(volume * gain[None], axis=1)
        for q in range(BLOCK):
            for t in range(ITERS):
                looked[t] = jnp.where(at_rho[t] == BLOCK * blk + q, volume[q], looked[t])

    levels = jnp.bitwise_and(iota((COLS, COLS), 1) - iota((COLS, COLS), 0), COLS - 1)
    valid = levels < lim[...]
    masked = jnp.where(valid, lg[...], -1e30)
    weights = jnp.where(valid, jnp.exp(masked - jnp.max(masked, axis=0, keepdims=True)), 0.0)
    moment = jnp.sum(weights * levels.astype(F32), axis=0, keepdims=True)
    disparity = moment / jnp.sum(weights, axis=0, keepdims=True) / 8.0

    high = disparity.astype(BF16).astype(F32)
    middle = (disparity - high).astype(BF16).astype(F32)
    low = disparity - high - middle
    sub8 = iota((8, COLS), 0)
    parts = jnp.zeros((8, COLS), F32)
    for i, piece in enumerate((high, middle, low)):
        parts = jnp.where(sub8 == i, piece, parts)
    lm[REACH, 1] = jnp.concatenate([looked[0], parts, looked[1], looked[2]], 0).astype(BF16)
    for r in reversed(order):
        start(looks, r)

    def side_by_side(ref, i):
        for b in range(3):
            x4[i, :, 128 * b : 128 * b + 128] = ref[i, 7 + b : 7 + b + EXT, :].astype(BF16)

    def taps_of(low, high, lanes):
        return jnp.concatenate(
            [
                x4[low - 1 + a : high - 1 + a, :, lanes].reshape((high - low) * EXT, -1)
                for a in range(3)
            ],
            1,
        )

    def chunks(low, high):
        half = (high - low + 1) // 2 if high - low > 5 else high - low
        return [(k, min(k + half, high)) for k in range(low, high, half)]

    for r in order:
        arrive(hids, r)
    for r in range(-REACH, REACH + 1):
        i = r + REACH
        hf[i, 16 : 16 + COLS, :] = jnp.where(row_ok[r], hr[i].astype(F32), 0.0)
        hf[i, 8:16, :] = jnp.where(row_ok[r] & left_ok, hl[i].astype(F32), 0.0)
        hf[i, 16 + COLS : 24 + COLS, :] = jnp.where(
            row_ok[r] & right_ok, hrt[i].astype(F32), 0.0
        )
        side_by_side(hf, i)
    hid_taps = jnp.concatenate([w4[512 * a : 512 * a + 384, 0:256] for a in range(3)], 0)
    for low, high in chunks(1, ROWS - 1):
        part[low:high] = dot(taps_of(low, high, slice(0, 384)), hid_taps).reshape(
            high - low, EXT, 256
        )
    lane_ext = iota((EXT, 128), 1)
    col = iota((EXT, 128), 0)
    inside = jnp.where(
        (col < 8) & jnp.logical_not(left_ok) | (col >= 8 + COLS) & jnp.logical_not(right_ok), 0.0, 1.0
    )

    lane32 = iota((32, COLS), 1)
    place = one_hot(iota((EXT, 256), 0) == iota((EXT, 256), 1))
    take = one_hot((iota((128, 128), 0) >= 40) & (iota((128, 128), 0) < 43))
    zero = jnp.zeros((32, COLS), F32)

    def inputs_of(i):
        inputs = lk3[i]
        for b in range(3):
            shifted = 0.25 * dd[i, 7 + b : 7 + b + EXT, :]
            inputs = jnp.where(lane_ext == 32 * b + 8, shifted, inputs)
        x4[i, :, 384:512] = inputs.astype(BF16)

    for groups in (feats, hids):
        for r in groups:
            leave(groups, r)
    def gates_of(t, spans):
        if t == 0:
            lanes = slice(384, 512)
            weights = jnp.concatenate([win[0, a, :, 0:256] for a in range(3)], 0)
        else:
            lanes, weights = slice(0, 512), w4[:, 0:256]
        gates = dot(
            jnp.concatenate([taps_of(first, last, lanes) for first, last in spans], 0), weights
        )
        at = 0
        for first, last in spans:
            size = last - first
            mine = gates[at * EXT : (at + size) * EXT].reshape(size, EXT, 256)
            if t == 0:
                mine = mine + part[first:last]
            up[first:last] = jax.nn.sigmoid(mine[:, :, 0:128])
            reset = jax.nn.sigmoid(mine[:, :, 128:256])
            rf[first:last, 8 : 8 + EXT, :] = reset * hf[first:last, 8 : 8 + EXT, :]
            at += size

    def states_of(t, spans):
        pre = dot(
            jnp.concatenate([taps_of(first, last, slice(0, 512)) for first, last in spans], 0),
            w4[:, 256:384],
        )
        at = 0
        for first, last in spans:
            size = last - first
            candidate = jnp.tanh(pre[at * EXT : (at + size) * EXT]).reshape(size, EXT, 128)
            update = up[first:last]
            fresh = (1.0 - update) * hf[first:last, 8 : 8 + EXT, :] + update * candidate
            for i in range(first, last):
                kept = fresh[i - first]
                if t < ITERS - 1:
                    kept = kept * (inside * flag(row_ok[i - REACH]))
                hf[i, 8 : 8 + EXT, :] = kept.astype(BF16).astype(F32)
            at += size

    def first_step(gate_spans, state_spans):
        gates_of(0, gate_spans)
        for first, last in gate_spans:
            for i in range(first, last):
                side_by_side(rf, i)
        states_of(0, state_spans)

    for a in range(3):
        w4[512 * a + 384 : 512 * a + 512, :] = win[0, a]
    for at, r in enumerate(order):
        if at == 9:
            first_step([(3, 10)], [(4, 9)])
        if at in (0, 5, 9):
            for other in order[at : {0: 5, 5: 9, 9: 13}[at]]:
                arrive(looks, other)
        i = r + REACH

        def tile(c, ok):
            if abs(r) <= 4:
                return jnp.where(ok, lm[i, c + 1].astype(F32), 0.0)
            return jnp.concatenate(
                [jnp.where(ok, lm[i, c + 1, 0:16].astype(F32), 0.0), zero[0:16]], 0
            )

        left, own, right = (
            tile(-1, row_ok[r] & left_ok), tile(0, row_ok[r]), tile(1, row_ok[r] & right_ok)
        )
        lows, highs = [], []
        for shift in (-1, 0, 1):
            lows.append(pltpu.roll(jnp.where(lane32 < 120 + shift, own, left), 8 - shift, 1))
            highs.append(pltpu.roll(jnp.where(lane32 < 120 + shift, right, own), 8 - shift, 1))
        wide = jnp.concatenate(
            [jnp.concatenate(lows + [zero], 0), jnp.concatenate(highs + [zero], 0)], 1
        ).astype(BF16)
        found = dot_nt(place, wide)
        lk3[i] = found
        dd[i, 8 : 8 + EXT, :] = dot(found.astype(BF16), take)
        inputs_of(i)

    for r in looks:
        leave(looks, r)

    first_step([(1, 3), (10, 12)], [(2, 4), (9, 11)])
    for t in range(ITERS):
        reach = REACH - 2 * t
        low, high = REACH - reach, REACH + reach + 1
        if t > 0:
            for a in range(3):
                w4[512 * a + 384 : 512 * a + 512, :] = win[t, a]
            for i in range(low, high):
                side_by_side(hf, i)
                dd[i, 8 : 8 + EXT, :] += dot(x4[i, :, 128:256], head)
                inputs_of(i)
            for span in chunks(low + 1, high - 1):
                gates_of(t, [span])
            for i in range(low + 1, high - 1):
                side_by_side(rf, i)
            for span in chunks(low + 2, high - 2):
                states_of(t, [span])
        own = hf[REACH, 16 : 16 + COLS, :].astype(BF16)
        disparity += dot_nt(head_row, own)[0:1]
    fin_h[...] = own
    c1 = pltpu.make_async_copy(fin_h, hid_out, local_sem.at[0])
    c1.start()
    fin_d[...] = disparity
    c2 = pltpu.make_async_copy(fin_d, disp_out, local_sem.at[1])
    c2.start()
    c1.wait()
    c2.wait()


def local(
    feat_left, feat_right, limit, indices, hidden_start,
    vol_kernel, group_gain, hid_kernel, in_kernel, head_weight,
):
    any_spec = pl.BlockSpec(memory_space=pl.ANY)
    dma = pltpu.SemaphoreType.DMA
    disparity, hidden = pl.pallas_call(
        kernel,
        out_shape=(
            jax.ShapeDtypeStruct((1, COLS), F32),
            jax.ShapeDtypeStruct((COLS, HID), BF16),
        ),
        in_specs=[any_spec] * 10,
        out_specs=(any_spec, any_spec),
        scratch_shapes=[
            pltpu.VMEM((3, CH, COLS), BF16),
            pltpu.VMEM((3, CH, COLS), BF16),
            pltpu.VMEM((3, CH, COLS), BF16),
            pltpu.VMEM((16, 128), BF16),
            pltpu.VMEM((3, 16, 128), BF16),
            pltpu.VMEM((3, 16, 128), BF16),
            pltpu.VMEM((1, COLS), jnp.int32),
            pltpu.VMEM((ITERS, 1, COLS), jnp.int32),
            pltpu.VMEM((216, 8), BF16),
            pltpu.VMEM((3, 9, 3, 384), BF16),
            pltpu.VMEM((1, HID), BF16),
            pltpu.VMEM((3, CH, 3 * COLS), BF16),
            pltpu.VMEM((2, COLS + 8, COLS), F32),
            pltpu.VMEM((8 * COLS + 16, 2 * COLS), BF16),
            pltpu.VMEM((8 * (COLS + 2), COLS), F32),
            pltpu.VMEM((3, 3, 8 * (COLS + 2), COLS), BF16),
            pltpu.VMEM((9 * WINDOW, COLS), BF16),
            pltpu.VMEM((128, 9 * WINDOW), BF16),
            pltpu.VMEM((COLS, COLS), F32),
            pltpu.VMEM((ROWS, COLS, HID), BF16),
            pltpu.VMEM((ROWS, 8, HID), BF16),
            pltpu.VMEM((ROWS, 8, HID), BF16),
            pltpu.VMEM((ROWS, 3, 32, COLS), BF16),
            pltpu.VMEM((ROWS, EXT + 16, 128), F32),
            pltpu.VMEM((ROWS, EXT + 16, 128), F32),
            pltpu.VMEM((ROWS, EXT + 16, 128), F32),
            pltpu.VMEM((ROWS, EXT, 128), F32),
            pltpu.VMEM((ROWS, EXT, 512), BF16),
            pltpu.VMEM((ROWS, EXT, 128), F32),
            pltpu.VMEM((ROWS, EXT, 256), F32),
            pltpu.VMEM((3 * 512, 384), BF16),
            pltpu.VMEM((ITERS, 3, 128, 384), BF16),
            pltpu.VMEM((3, 32, 384), F32),
            dma((12,)),
            dma((13,)),
            dma((13,)),
            dma((3 * ROWS - 1,)),
            dma((3 * ROWS - 1,)),
            dma((3 * ROWS - 1,)),
            dma((3 * ROWS - 1,)),
            pltpu.SemaphoreType.REGULAR((3,)),
            pltpu.VMEM((COLS, HID), BF16),
            pltpu.VMEM((1, COLS), F32),
            pltpu.SMEM((GROUPS,), F32),
        ],
        compiler_params=pltpu.CompilerParams(collective_id=0, has_side_effects=True, vmem_limit_bytes=40*2**20),
        name="stereo",
    )(
        *[
            pltpu.with_memory_space_constraint(x, pltpu.HBM)
            for x in (
                group_gain,
                feat_left[0],
                feat_right[0],
                limit,
                indices,
                hidden_start[0],
                vol_kernel.reshape(216, 8),
                hid_kernel.reshape(3, 384, 384),
                in_kernel.transpose(0, 2, 1, 3),
                head_weight.reshape(1, HID),
            )
        ],
    )
    return disparity, hidden[None]


def solution(mesh):
    in_specs = (
        P("band", None, "disp"),
        P("band", None, "disp"),
        P("band", "disp"),
        P(None, "band", "disp"),
        P("band", "disp", None),
        P(),
        P(),
        P(),
        P(),
        P(),
    )
    out_specs = (P("band", "disp"), P("band", "disp", None))
    return jax.shard_map(local, mesh=mesh, in_specs=in_specs, out_specs=out_specs, check_vma=False)
```
